32 devices in a mesh: segment: 2 (over core), expert: 16 (over z, y, x).
Axes of the slice: x: 2, y: 2, z: 4, core: 2. Of those that a mesh axis runs over, the one named last changes fastest.
Arguments:
- rollout: bfloat16 [2048, 4096], P('expert', 'segment'), may hold values from -6 to 6
- norm_gain: bfloat16 [2, 4096], P('segment'), may hold values from 0.25 to 1.75
- router_first: bfloat16 [2, 4096, 28], P('segment')
- gain_second: bfloat16 [2, 4096], P('segment'), may hold values from 0.25 to 1.75
- router_second: bfloat16 [2, 4096, 28], P('segment')
- expert_ids: int32 [2048, 8], P('expert'), may hold values from 0 to 27, as said below
- copy_pick: int32 [2048, 8], P('expert'), may hold values from 0 to 5
- later_ids: int32 [2048, 8], P('expert'), may hold values from 0 to 27, all different within a row
- slot_table: int32 [32], replicated, may hold values from 0 to 27, as said below
- expert_in: bfloat16 [32, 4096, 1536], P(('segment', 'expert'))
- expert_out: bfloat16 [32, 768, 4096], P(('segment', 'expert'))
Outputs:
- states: bfloat16 [2, 2048, 4096], P('segment', 'expert')
- log_ratio: float32 [1024, 2], P('expert', 'segment')
The draws below stay inside these ranges and needn't reach their ends.
Inputs may be any that keep to these rules, and one draw needn't show every extreme that they name: `expert_ids`: each row names 8 different experts. `slot_table`: every expert is held by one, two or three slots.
All inputs are finite; a program needn't handle non-finite values.
Results may differ from the reference program's by a relative error of at most 0.013.
The reference program's roundings to bfloat16 on the way count: a program that leaves them out, or rounds other values in their place, can miss the bound.
Values may be sent and summed in bfloat16 or wider, within the bound.
A program may use at most 192 MiB of HBM per device.

```python
import jax
import jax.numpy as jnp
from jax import lax

D = 4096
FF = 768
TOP = 8
TOK_DEV = 128
SLOTS = 32
HOT = 2
EXPERTS = 28
CAP = 48
TOKENS = 2048
N_EXPERT = 16


def slot_plan(key):
    hot = jax.random.permutation(jax.random.fold_in(key, 11), EXPERTS)[:HOT].astype(jnp.int32)
    base = jnp.concatenate([jnp.arange(EXPERTS, dtype=jnp.int32), hot, hot])
    order = jax.random.permutation(jax.random.fold_in(key, 12), SLOTS)
    table = base[order].astype(jnp.int32)
    is_hot = jnp.sum((jnp.arange(EXPERTS, dtype=jnp.int32)[:, None] == hot[None, :]).astype(jnp.int32), axis=1)
    return (table, is_hot)


def draw_slot_table(key, part):
    return slot_plan(key)[0]


def draw_expert_ids(key, part):
    table, is_hot = slot_plan(key)
    scores = jax.random.randint(jax.random.fold_in(key, 13), (TOKENS, EXPERTS), 0, 1000) + 200 * is_hot[None, :]
    ranks = jax.random.permutation(jax.random.fold_in(key, 14), EXPERTS).astype(jnp.int32)
    distinct = scores * EXPERTS + ranks[None, :]
    return lax.top_k(distinct, TOP)[1].astype(jnp.int32)


def expert_draw(key, salt, rows, cols):
    table = slot_plan(key)[0]
    base = jax.random.fold_in(key, salt)

    def one(expert):
        values = jax.random.normal(jax.random.fold_in(base, expert), (rows, cols), jnp.float32)
        return (values * rows ** (-0.5)).astype(jnp.bfloat16)
    return lax.map(one, table)


def draw_expert_in(key, part):
    return expert_draw(key, 21, D, 2 * FF)


def draw_expert_out(key, part):
    return expert_draw(key, 22, FF, D)


def router_draw(key, salt):
    values = jax.random.normal(jax.random.fold_in(key, salt), (2, D, EXPERTS), jnp.float32) * D ** (-0.5)
    spread = jax.random.uniform(jax.random.fold_in(key, salt + 1), (2, 1, EXPERTS), jnp.float32, 0.5, 2.5)
    values = values * spread
    return values.astype(jnp.bfloat16)


def draw_router_first(key, part):
    return router_draw(key, 31)


def draw_router_second(key, part):
    return router_draw(key, 41)


def plant(values, key, least, top_value):
    place = [jax.random.randint(jax.random.fold_in(key, axis), (), 0, length) for axis, length in enumerate(values.shape)]
    main_axis = values.shape.index(max(values.shape))
    next_to = place[:main_axis] + [(place[main_axis] + 1) % values.shape[main_axis]] + place[main_axis + 1:]
    return values.at[tuple(place)].set(least).at[tuple(next_to)].set(top_value)


def block_scale(rng, dims, shards, low, high):
    level = 1.0
    for position, blocks in shards:
        steps = jax.random.uniform(jax.random.fold_in(jax.random.fold_in(rng, 6), position), (blocks,), jnp.float32, low / len(shards), high / len(shards))
        level = level * jnp.repeat(jnp.exp(steps), dims[position] // blocks).reshape((-1,) + (1,) * (len(dims) - 1 - position))
    return level


def choose_distinct(own_key, rows, number_of, top, lift):
    ranking = jax.random.permutation(jax.random.fold_in(own_key, 1), number_of)
    pull = ranking
    for power in range(3):
        pull = pull * pull // number_of
    pull = pull * lift // number_of
    lots = jax.random.randint(jax.random.fold_in(own_key, 2), (rows, number_of), 0, 4096) + pull
    sure = jax.random.permutation(jax.random.fold_in(own_key, 3), rows)[jnp.arange(number_of) % rows]
    lots = jnp.where(jnp.arange(rows)[:, None] == sure[None, :], 1 << 14, lots)
    score = lots * number_of + jnp.arange(number_of)
    return lax.top_k(score.astype(jnp.int32), top)[1].astype(jnp.int32)


def scatter_about(key, dims, scale, most, pieces=(), held_as=jnp.bfloat16):
    level = block_scale(key, dims, pieces, -0.22, 0.18) if pieces else 1.0
    values = jax.random.normal(key, dims, jnp.float32) * scale * level
    return jnp.minimum(jnp.maximum(values, -most), most).astype(held_as)


def setup_inputs(seed: int = 0) -> dict:
    key_list = jax.random.split(jax.random.key(seed), 12)
    rollout = scatter_about(key_list[0], (TOKENS, D), 1.0, 6.0, ((0, 16), (1, 2)))
    norm_gain = jnp.clip(1.0 + 0.15 * jax.random.normal(key_list[1], (2, D), jnp.float32), 0.25, 1.75).astype(jnp.bfloat16)
    router_first = draw_router_first(jax.random.fold_in(key_list[11], 71), 0)
    gain_second = jnp.clip(1.0 + 0.15 * jax.random.normal(key_list[3], (2, D), jnp.float32), 0.25, 1.75).astype(jnp.bfloat16)
    router_second = draw_router_second(jax.random.fold_in(key_list[11], 71), 0)
    expert_ids = draw_expert_ids(jax.random.fold_in(key_list[11], 71), 0)
    copy_pick = plant(jax.random.randint(key_list[6], (TOKENS, TOP), 0, 6), jax.random.fold_in(key_list[6], 1), 0, 5).astype(jnp.int32)
    later_ids = choose_distinct(key_list[7], TOKENS, EXPERTS, TOP, 2340)
    slot_table = draw_slot_table(jax.random.fold_in(key_list[11], 71), 0)
    expert_in = draw_expert_in(jax.random.fold_in(key_list[11], 71), 0)
    expert_out = draw_expert_out(jax.random.fold_in(key_list[11], 71), 0)
    return dict(rollout=rollout, norm_gain=norm_gain, router_first=router_first, gain_second=gain_second, router_second=router_second, expert_ids=expert_ids, copy_pick=copy_pick, later_ids=later_ids, slot_table=slot_table, expert_in=expert_in, expert_out=expert_out)


def rms_scale(values, gain):
    return values * lax.rsqrt(lax.optimization_barrier(jnp.mean(values * values, axis=-1, keepdims=True)) + 1e-06) * gain.astype(jnp.float32)

def slot_routes(expert_ids, copy_pick, slot_table):
    slot_ids = jnp.arange(SLOTS, dtype=jnp.int32)
    same = slot_table[:, None] == slot_table[None, :]
    earlier = slot_ids[:, None] < slot_ids[None, :]
    copy_rank = lax.optimization_barrier(jnp.sum((same & earlier).astype(jnp.int32), axis=0))
    holders = lax.optimization_barrier(jnp.sum((slot_table[None, :] == jnp.arange(EXPERTS, dtype=jnp.int32)[:, None]).astype(jnp.int32), axis=1))
    picked = (expert_ids[..., None] == jnp.arange(EXPERTS, dtype=jnp.int32)).astype(jnp.int32)
    copies = lax.optimization_barrier(jnp.sum(picked * holders, axis=-1))
    wanted = copy_pick % copies
    match = ((slot_table == expert_ids[..., None]) & (copy_rank == wanted[..., None])).astype(jnp.int32)
    slot = lax.optimization_barrier(jnp.sum(match * slot_ids, axis=-1)).astype(jnp.int32)
    return (slot, match)

def reference(rollout, norm_gain, router_first, gain_second, router_second, expert_ids, copy_pick, later_ids, slot_table, expert_in, expert_out):
    states_in = rollout.astype(jnp.float32)
    slot, match = slot_routes(expert_ids, copy_pick, slot_table)
    blocks = match.reshape(N_EXPERT, TOK_DEV * TOP, SLOTS)
    before = jnp.cumsum(blocks, axis=1) - blocks
    rank = lax.optimization_barrier(jnp.sum(before * blocks, axis=-1)).reshape(TOKENS, TOP).astype(jnp.int32)
    kept = rank < CAP
    rank_c = jnp.where(kept, rank, CAP).astype(jnp.int32)
    token_ids = jnp.arange(TOKENS, dtype=jnp.int32)
    source = jnp.broadcast_to((token_ids // TOK_DEV)[:, None], (TOKENS, TOP)).astype(jnp.int32)
    local = jnp.broadcast_to((token_ids % TOK_DEV)[:, None], (TOKENS, TOP)).astype(jnp.int32)
    normed_all = []
    gates_all = []
    for section in range(2):
        normed = rms_scale(states_in, norm_gain[section]).astype(jnp.bfloat16)
        logits = jnp.dot(normed, router_first[section], preferred_element_type=jnp.float32)
        chosen = jnp.take_along_axis(logits, expert_ids, axis=1)
        lifted = jnp.exp(chosen - lax.optimization_barrier(jnp.max(chosen, axis=1, keepdims=True)))
        gates = (lifted / lax.optimization_barrier(jnp.sum(lifted, axis=1, keepdims=True))).astype(jnp.bfloat16)
        normed_all.append(normed)
        gates_all.append(gates)
    normed_all = jnp.stack(normed_all)
    gates_all = jnp.stack(gates_all).astype(jnp.float32)
    inverse = jnp.full((N_EXPERT, SLOTS, CAP), TOK_DEV, jnp.int32).at[source, slot, rank_c].set(local, mode='drop')
    gate_slots = jnp.zeros((2, N_EXPERT, SLOTS, CAP), jnp.float32).at[:, source, slot, rank_c].set(gates_all, mode='drop')
    padded = jnp.concatenate([normed_all.reshape(2, N_EXPERT, TOK_DEV, D), jnp.zeros((2, N_EXPERT, 1, D), jnp.bfloat16)], axis=2)
    block_ids = jnp.arange(N_EXPERT, dtype=jnp.int32)[:, None]

    def one_slot(total, inputs):
        index, weight, w_in, w_out = inputs
        rows = padded[:, block_ids, index]
        hidden = jnp.dot(rows.reshape(-1, D), w_in, preferred_element_type=jnp.float32)
        active = (jax.nn.silu(hidden[:, :FF]) * hidden[:, FF:]).astype(jnp.bfloat16)
        result = jnp.dot(active, w_out, preferred_element_type=jnp.float32).astype(jnp.bfloat16)
        result = lax.optimization_barrier(result).astype(jnp.float32).reshape(2, N_EXPERT, CAP, D)
        total = total.at[:, block_ids, index].add(weight[..., None] * result)
        return (total, None)
    start = jnp.zeros((2, N_EXPERT, TOK_DEV + 1, D), jnp.float32)
    total, _ = lax.scan(one_slot, start, (inverse.transpose(1, 0, 2), gate_slots.transpose(2, 0, 1, 3), expert_in, expert_out))
    mixed = states_in[None] + total[:, :, :TOK_DEV].reshape(2, TOKENS, D)
    states = mixed.astype(jnp.bfloat16)
    scores = []
    for section in range(2):
        later = rms_scale(mixed[section], gain_second[section]).astype(jnp.bfloat16)
        logits = jnp.dot(later, router_second[section], preferred_element_type=jnp.float32)
        logp = jax.nn.log_softmax(logits, axis=-1)
        scores.append(lax.optimization_barrier(jnp.sum(jnp.take_along_axis(logp, later_ids, axis=1), axis=1)))
    return (states, (scores[1] - scores[0]).reshape(TOKENS // 2, 2))
```

```python
import jax
import jax.numpy as jnp
from jax import lax
from jax.sharding import PartitionSpec as P

CHUNKS = 2


def swap_cores(x):
    count = lax.axis_size("segment")
    return lax.ppermute(x, "segment", [(i, count - 1 - i) for i in range(count)])


def inverse_rms(values):
    return lax.rsqrt(jnp.mean(values * values, axis=-1, keepdims=True) + 1e-06)


def per_device(
    rollout,
    norm_gain,
    router_first,
    gain_second,
    router_second,
    expert_ids,
    copy_pick,
    later_ids,
    slot_table,
    expert_in,
    expert_out,
):
    position = lax.axis_index("segment")
    segment_count = lax.axis_size("segment")
    chip_count = lax.axis_size("expert")
    tok_rows, half = rollout.shape
    top_count = expert_ids.shape[1]
    experts_all = router_first.shape[2]
    slot_count = slot_table.shape[0]
    capacity = 3 * tok_rows * top_count // (2 * segment_count * chip_count)
    hidden_units = expert_out.shape[1]
    width = expert_out.shape[2]

    everyone = lax.all_gather(rollout, "expert", axis=0)

    expert_cols = jnp.arange(experts_all, dtype=jnp.int32)
    slot_ids = jnp.arange(slot_count, dtype=jnp.int32)
    same = slot_table[:, None] == slot_table[None, :]
    earlier = slot_ids[:, None] < slot_ids[None, :]
    copy_rank = jnp.sum((same & earlier).astype(jnp.int32), axis=0)
    slot_holders = jnp.sum(same.astype(jnp.int32), axis=0)
    here = slot_table == expert_ids[..., None]
    copies = jnp.max(jnp.where(here, slot_holders, 1), axis=-1)
    wanted = copy_pick % copies
    match = here & (copy_rank == wanted[..., None])
    hit = jnp.sum(match.astype(jnp.bfloat16), axis=1)
    order = jnp.arange(tok_rows, dtype=jnp.int32)
    before_mask = (order[None, :] < order[:, None]).astype(jnp.bfloat16)
    before = jnp.dot(before_mask, hit, preferred_element_type=jnp.float32).astype(jnp.int32)
    place = jnp.where(before < capacity, slot_ids * capacity + before, -1)
    target = jnp.sum(jnp.where(match, place[:, None, :], 0), axis=-1)
    targets = lax.all_gather(target, "expert", axis=0)

    other_half = swap_cores(rollout)
    first = position == 0
    left = jnp.where(first, rollout, other_half)
    right = jnp.where(first, other_half, rollout)
    whole = jnp.concatenate([left, right], axis=1)
    states_in = whole.astype(jnp.float32)
    normed = (states_in * inverse_rms(states_in) * norm_gain[0].astype(jnp.float32)).astype(
        jnp.bfloat16
    )
    logits = jnp.dot(normed, router_first[0], preferred_element_type=jnp.float32)
    picked = expert_ids[..., None] == expert_cols
    chosen = jnp.sum(jnp.where(picked, logits[:, None, :], 0.0), axis=-1)
    lifted = jnp.exp(chosen - jnp.max(chosen, axis=1, keepdims=True))
    gates = (lifted / jnp.sum(lifted, axis=1, keepdims=True)).astype(jnp.bfloat16)
    gates_all = lax.all_gather(gates, "expert", axis=0).astype(jnp.float32)

    chip = lax.axis_index("expert")
    own_base = (position * chip_count + chip) * capacity
    other_base = ((segment_count - 1 - position) * chip_count + chip) * capacity

    def places_in(base):
        inside = (targets >= base) & (targets < base + capacity)
        place = jnp.sum(jnp.where(inside, targets - base + 1, 0), axis=-1) - 1
        weight = jnp.sum(jnp.where(inside, gates_all, 0.0), axis=-1)
        return place, weight

    own_place, own_weight = places_in(own_base)
    other_place, other_weight = places_in(other_base)
    rows = jnp.arange(capacity, dtype=jnp.int32)

    def pick_rows(place):
        onehot = (place[:, None, :] == rows[None, :, None]).astype(jnp.bfloat16)
        got = jnp.einsum("sct,std->scd", onehot, everyone, preferred_element_type=jnp.float32)
        return got.astype(jnp.bfloat16).reshape(chip_count * capacity, half)

    other_rows = swap_cores(pick_rows(other_place))
    own_rows = pick_rows(own_place)
    left = jnp.where(first, own_rows, other_rows)
    right = jnp.where(first, other_rows, own_rows)
    full = jnp.concatenate([left, right], axis=1).astype(jnp.float32)
    scaled = full * inverse_rms(full)
    other_gain = swap_cores(norm_gain)
    inputs = jnp.concatenate(
        [
            (scaled * gain[0].astype(jnp.float32)).astype(jnp.bfloat16)
            for gain in (other_gain, norm_gain)
        ],
        axis=0,
    )
    hidden = jnp.dot(inputs, expert_in[0], preferred_element_type=jnp.float32)
    active = (jax.nn.silu(hidden[:, :hidden_units]) * hidden[:, hidden_units:]).astype(jnp.bfloat16)

    def spread(place, weight):
        return jnp.where(place[..., None] == rows, weight[..., None], 0.0).astype(jnp.bfloat16)

    weights = jnp.concatenate(
        [spread(own_place, own_weight), spread(other_place, other_weight)], axis=2
    )
    slot_rows = chip_count * capacity
    piece = width // CHUNKS
    parts = []
    for c in range(CHUNKS):
        w_out = expert_out[0, :, c * piece : (c + 1) * piece]
        result = jnp.dot(active, w_out, preferred_element_type=jnp.float32).astype(jnp.bfloat16)
        theirs = swap_cores(result[:slot_rows]).reshape(chip_count, capacity, piece)
        mine = result[slot_rows:].reshape(chip_count, capacity, piece)
        both = jnp.concatenate([mine, theirs], axis=1)
        given = jnp.einsum("stc,scd->std", weights, both, preferred_element_type=jnp.float32)
        given = given.astype(jnp.bfloat16).reshape(chip_count * tok_rows, piece)
        parts.append(lax.psum_scatter(given, "expert", scatter_dimension=0, tiled=True))
    mixed = states_in + jnp.concatenate(parts, axis=1).astype(jnp.float32)
    later = (mixed * inverse_rms(mixed) * gain_second[0].astype(jnp.float32)).astype(jnp.bfloat16)
    logp = jax.nn.log_softmax(
        jnp.dot(later, router_second[0], preferred_element_type=jnp.float32), axis=-1
    )
    later_pick = later_ids[..., None] == expert_cols
    score = jnp.sum(jnp.where(later_pick, logp[:, None, :], 0.0), axis=(1, 2))
    partner = swap_cores(score)
    ratio = jnp.where(position == 1, score - partner, partner - score)
    paired = ratio.reshape(tok_rows // 2, 2)
    column = lax.dynamic_slice_in_dim(paired, position, 1, 1)
    return (mixed.astype(jnp.bfloat16)[None], column)


def solution(mesh):
    in_specs = (
        P("expert", "segment"),
        P("segment", None),
        P("segment", None, None),
        P("segment", None),
        P("segment", None, None),
        P("expert", None),
        P("expert", None),
        P("expert", None),
        P(),
        P(("segment", "expert"), None, None),
        P(("segment", "expert"), None, None),
    )
    out_specs = (P("segment", "expert", None), P("expert", "segment"))
    return jax.shard_map(
        per_device, mesh=mesh, in_specs=in_specs, out_specs=out_specs, check_vma=False
    )
```

```python
import functools
import math

import jax
import jax.numpy as jnp
from jax import lax
from jax.experimental import pallas as pl
from jax.experimental.pallas import tpu as pltpu
from jax.sharding import PartitionSpec as P

LANES = 128
VMEM_BUDGET = 24 << 20
MESH = pl.DeviceIdType.MESH


def grid_sides(count):
    outer = 1
    while outer**3 < count:
        outer *= 2
    rest = count // outer
    middle = 1
    while middle**2 < rest:
        middle *= 2
    return outer, middle, rest // middle


def return_kernel(sides, chunks, act, w_out, wts, out, mine, give, got, *rest):
    n_a, n_b, n_c = sides
    bufs, sems = rest[:12], rest[12:]
    seg = lax.axis_index("segment")
    me = lax.axis_index("expert")
    a, b, c = me // (n_b * n_c), (me // n_c) % n_b, me % n_c
    blocks = n_a * n_b * n_c
    slot_rows = mine.shape[1]
    cap = slot_rows // blocks
    wide = mine.shape[2]
    half = wide // 2
    tile = math.gcd(slot_rows, 256)

    def at(na, nb, nc):
        return (seg, (na * n_b + nb) * n_c + nc)

    partner = (1 - seg, me)

    def peer_a(k):
        return at((a + k) % n_a, b, c)

    def peer_b(k):
        return at(a, (b + k) % n_b, c)

    def peer_c(k):
        return at(a, b, (c + k) % n_c)

    barrier = pltpu.get_barrier_semaphore()
    friends = [partner]
    friends += [peer_a(k) for k in range(1, n_a)]
    friends += [peer_b(k) for k in range(1, n_b)]
    friends += [peer_c(k) for k in range(1, n_c)]
    for friend in friends:
        pl.semaphore_signal(barrier, inc=1, device_id=friend, device_id_type=MESH)
    pl.semaphore_wait(barrier, len(friends))

    orders = (
        ((c, n_c, peer_c), (b, n_b, peer_b)),
        ((b, n_b, peer_b), (c, n_c, peer_c)),
    )

    def swap(j):
        return pltpu.make_async_remote_copy(
            src_ref=give.at[j % 2],
            dst_ref=got.at[j],
            send_sem=sems[0].at[j % 2],
            recv_sem=sems[1].at[j],
            device_id=partner,
            device_id_type=MESH,
        )

    def sends(half_index, phase, j):
        first, second = orders[half_index]
        src, dst = bufs[half_index * 6 + phase * 2 : half_index * 6 + phase * 2 + 2]
        send, recv = sems[2 + half_index * 6 + phase * 2 : 4 + half_index * 6 + phase * 2]
        place, side, peer = (first, second, (a, n_a, peer_a))[phase]
        return [
            pltpu.make_async_remote_copy(
                src_ref=src.at[j % 2, (place + k) % side],
                dst_ref=dst.at[j, k - 1],
                send_sem=send.at[j % 2, k - 1],
                recv_sem=recv.at[j, k - 1],
                device_id=peer(k),
                device_id_type=MESH,
            )
            for k in range(1, side)
        ]

    def project(j):
        columns = pl.ds(pl.multiple_of(j * wide, wide), wide)

        def one(r, dest, base):
            rows = pl.ds(pl.multiple_of(r * tile, tile), tile)
            source = pl.ds(pl.multiple_of(base + r * tile, tile), tile)
            dest[j % 2, rows, :] = jnp.dot(
                act[source, :], w_out[:, columns], preferred_element_type=jnp.float32
            ).astype(jnp.bfloat16)

        @pl.loop(0, slot_rows // tile)
        def _(r):
            one(r, give, 0)

        swap(j).start()

        @pl.loop(0, slot_rows // tile)
        def _(r):
            one(r, mine, slot_rows)

    def spread(j):
        swap(j).wait()

        @pl.loop(0, blocks)
        def _(d):
            da, db, dc = d // (n_b * n_c), (d // n_c) % n_b, d % n_c
            rows = pl.ds(pl.multiple_of(d * cap, cap), cap)
            both = jnp.concatenate([mine[j % 2, rows, :], got[j, rows, :]], axis=0)
            part = jnp.dot(wts[d], both, preferred_element_type=jnp.float32)
            part = part.astype(jnp.bfloat16)
            bufs[0][j % 2, dc, db * n_a + da] = part[:, :half]
            bufs[6][j % 2, db, dc * n_a + da] = part[:, half:]

        for half_index in range(2):
            for copy in sends(half_index, 0, j):
                copy.start()

    def first_sum(j):
        for half_index in range(2):
            (place, side, _), (_, side2, _) = orders[half_index]
            src, dst, nxt = bufs[half_index * 6 : half_index * 6 + 3]
            for copy in sends(half_index, 0, j):
                copy.wait()

            @pl.loop(0, side2 * n_a)
            def _(d):
                total = src[j % 2, place, d].astype(jnp.float32)
                for k in range(side - 1):
                    total += dst[j, k, d].astype(jnp.float32)
                nxt[j % 2, d // n_a, d % n_a] = total.astype(jnp.bfloat16)

            for copy in sends(half_index, 1, j):
                copy.start()

    def second_sum(j):
        for half_index in range(2):
            place, side, _ = orders[half_index][1]
            src, dst, nxt = bufs[half_index * 6 + 2 : half_index * 6 + 5]
            for copy in sends(half_index, 1, j):
                copy.wait()

            @pl.loop(0, n_a)
            def _(d):
                total = src[j % 2, place, d].astype(jnp.float32)
                for k in range(side - 1):
                    total += dst[j, k, d].astype(jnp.float32)
                nxt[j % 2, d] = total.astype(jnp.bfloat16)

            for copy in sends(half_index, 2, j):
                copy.start()

    def last_sum(j):
        for half_index in range(2):
            src, dst = bufs[half_index * 6 + 4 : half_index * 6 + 6]
            for copy in sends(half_index, 2, j):
                copy.wait()
            total = src[j % 2, a].astype(jnp.float32)
            for k in range(n_a - 1):
                total += dst[j, k].astype(jnp.float32)
            columns = pl.ds(pl.multiple_of(j * wide + half_index * half, half), half)
            out[:, columns] = total

    stages = (project, spread, first_sum, second_sum, last_sum)

    @pl.loop(0, chunks + len(stages) - 1)
    def _(step):
        for lag, stage in enumerate(stages):

            @pl.when((step >= lag) & (step - lag < chunks))
            def _():
                stage(step - lag)


def return_call(sides, act, w_out, wts):
    n_a, n_b, n_c = sides
    tok_rows = wts.shape[1]
    slot_rows = act.shape[0] // 2
    half, wide = LANES, 2 * LANES
    block_bytes = tok_rows * half * 2
    chunk_bytes = slot_rows * wide * 2
    for first, second in ((n_c, n_b), (n_b, n_c)):
        chunk_bytes += block_bytes * n_a * (second * (first - 1) + second - 1)
        chunk_bytes += block_bytes * (n_a - 1)
    chunks = w_out.shape[1] // wide
    while chunks % 2 == 0 and chunks * chunk_bytes > VMEM_BUDGET:
        chunks //= 2

    def bf(*shape):
        return pltpu.VMEM(shape, jnp.bfloat16)

    def dma(*shape):
        return pltpu.SemaphoreType.DMA(shape)

    scratch = [bf(2, slot_rows, wide), bf(2, slot_rows, wide), bf(chunks, slot_rows, wide)]
    sems = [dma(2), dma(chunks)]
    for first, second in ((n_c, n_b), (n_b, n_c)):
        scratch += [
            bf(2, first, second * n_a, tok_rows, half),
            bf(chunks, first - 1, second * n_a, tok_rows, half),
            bf(2, second, n_a, tok_rows, half),
            bf(chunks, second - 1, n_a, tok_rows, half),
            bf(2, n_a, tok_rows, half),
            bf(chunks, n_a - 1, tok_rows, half),
        ]
        for side in (first, second, n_a):
            sems += [dma(2, side - 1), dma(chunks, side - 1)]
    piece = chunks * wide
    call = pl.pallas_call(
        functools.partial(return_kernel, sides, chunks),
        out_shape=jax.ShapeDtypeStruct((tok_rows, piece), jnp.float32),
        in_specs=[pl.BlockSpec(memory_space=pltpu.VMEM)] * 3,
        out_specs=pl.BlockSpec(memory_space=pltpu.VMEM),
        scratch_shapes=scratch + sems,
        compiler_params=pltpu.CompilerParams(
            collective_id=0, has_side_effects=True, vmem_limit_bytes=60 * 1024 * 1024
        ),
        name="return_sum",
    )
    parts = [
        call(act, w_out[:, start : start + piece], wts)
        for start in range(0, w_out.shape[1], piece)
    ]
    return parts[0] if len(parts) == 1 else jnp.concatenate(parts, axis=1)


def swap_cores(x):
    count = lax.axis_size("segment")
    return lax.ppermute(x, "segment", [(i, count - 1 - i) for i in range(count)])


def inverse_rms(values):
    return lax.rsqrt(jnp.mean(values * values, axis=-1, keepdims=True) + 1e-06)


def per_device(
    rollout,
    norm_gain,
    router_first,
    gain_second,
    router_second,
    expert_ids,
    copy_pick,
    later_ids,
    slot_table,
    expert_in,
    expert_out,
):
    position = lax.axis_index("segment")
    segment_count = lax.axis_size("segment")
    chip_count = lax.axis_size("expert")
    tok_rows, half = rollout.shape
    top_count = expert_ids.shape[1]
    experts_all = router_first.shape[2]
    slot_count = slot_table.shape[0]
    capacity = 3 * tok_rows * top_count // (2 * segment_count * chip_count)
    hidden_units = expert_out.shape[1]

    everyone = lax.all_gather(rollout, "expert", axis=0)

    expert_cols = jnp.arange(experts_all, dtype=jnp.int32)
    slot_ids = jnp.arange(slot_count, dtype=jnp.int32)
    same = slot_table[:, None] == slot_table[None, :]
    earlier = slot_ids[:, None] < slot_ids[None, :]
    copy_rank = jnp.sum((same & earlier).astype(jnp.int32), axis=0)
    slot_holders = jnp.sum(same.astype(jnp.int32), axis=0)
    here = slot_table == expert_ids[..., None]
    copies = jnp.max(jnp.where(here, slot_holders, 1), axis=-1)
    wanted = copy_pick % copies
    match = here & (copy_rank == wanted[..., None])
    hit = jnp.sum(match.astype(jnp.bfloat16), axis=1)
    order = jnp.arange(tok_rows, dtype=jnp.int32)
    before_mask = (order[None, :] < order[:, None]).astype(jnp.bfloat16)
    before = jnp.dot(before_mask, hit, preferred_element_type=jnp.float32).astype(jnp.int32)
    place = jnp.where(before < capacity, slot_ids * capacity + before, -1)
    target = jnp.sum(jnp.where(match, place[:, None, :], 0), axis=-1)
    other_half = swap_cores(rollout)
    first = position == 0
    left = jnp.where(first, rollout, other_half)
    right = jnp.where(first, other_half, rollout)
    whole = jnp.concatenate([left, right], axis=1)
    states_in = whole.astype(jnp.float32)
    normed = (states_in * inverse_rms(states_in) * norm_gain[0].astype(jnp.float32)).astype(
        jnp.bfloat16
    )
    logits = jnp.dot(normed, router_first[0], preferred_element_type=jnp.float32)
    picked = expert_ids[..., None] == expert_cols
    chosen = jnp.sum(jnp.where(picked, logits[:, None, :], 0.0), axis=-1)
    lifted = jnp.exp(chosen - jnp.max(chosen, axis=1, keepdims=True))
    gates = (lifted / jnp.sum(lifted, axis=1, keepdims=True)).astype(jnp.bfloat16)
    packed = jnp.concatenate([target.astype(jnp.float32), gates.astype(jnp.float32)], axis=1)
    packed = lax.all_gather(packed, "expert", axis=0)
    targets = packed[..., :top_count].astype(jnp.int32)
    gates_all = packed[..., top_count:]

    chip = lax.axis_index("expert")
    own_base = (position * chip_count + chip) * capacity
    other_base = ((segment_count - 1 - position) * chip_count + chip) * capacity

    def places_in(base):
        inside = (targets >= base) & (targets < base + capacity)
        place = jnp.sum(jnp.where(inside, targets - base + 1, 0), axis=-1) - 1
        weight = jnp.sum(jnp.where(inside, gates_all, 0.0), axis=-1)
        return place, weight

    own_place, own_weight = places_in(own_base)
    other_place, other_weight = places_in(other_base)
    room = -(-capacity // 16) * 16
    rows = jnp.arange(room, dtype=jnp.int32)

    def pick_rows(place):
        onehot = (place[:, None, :] == rows[None, :, None]).astype(jnp.bfloat16)
        got = jnp.einsum("sct,std->scd", onehot, everyone, preferred_element_type=jnp.float32)
        return got.astype(jnp.bfloat16).reshape(chip_count * room, half)

    other_rows = swap_cores(pick_rows(other_place))
    own_rows = pick_rows(own_place)
    left = jnp.where(first, own_rows, other_rows)
    right = jnp.where(first, other_rows, own_rows)
    full = jnp.concatenate([left, right], axis=1).astype(jnp.float32)
    scaled = full * inverse_rms(full)
    other_gain = swap_cores(norm_gain)
    inputs = jnp.concatenate(
        [
            (scaled * gain[0].astype(jnp.float32)).astype(jnp.bfloat16)
            for gain in (other_gain, norm_gain)
        ],
        axis=0,
    )
    hidden = jnp.dot(inputs, expert_in[0], preferred_element_type=jnp.float32)
    active = (jax.nn.silu(hidden[:, :hidden_units]) * hidden[:, hidden_units:]).astype(jnp.bfloat16)

    def spread(place, weight):
        return jnp.where(place[..., None] == rows, weight[..., None], 0.0).astype(jnp.bfloat16)

    weights = jnp.concatenate(
        [spread(own_place, own_weight), spread(other_place, other_weight)], axis=2
    )
    summed = return_call(grid_sides(chip_count), active, expert_out[0], weights)
    mixed = states_in + summed
    later = (mixed * inverse_rms(mixed) * gain_second[0].astype(jnp.float32)).astype(jnp.bfloat16)
    logp = jax.nn.log_softmax(
        jnp.dot(later, router_second[0], preferred_element_type=jnp.float32), axis=-1
    )
    later_pick = later_ids[..., None] == expert_cols
    score = jnp.sum(jnp.where(later_pick, logp[:, None, :], 0.0), axis=(1, 2))
    partner = swap_cores(score)
    ratio = jnp.where(position == 1, score - partner, partner - score)
    paired = ratio.reshape(tok_rows // 2, 2)
    column = lax.dynamic_slice_in_dim(paired, position, 1, 1)
    return (mixed.astype(jnp.bfloat16)[None], column)


def solution(mesh):
    in_specs = (
        P("expert", "segment"),
        P("segment", None),
        P("segment", None, None),
        P("segment", None),
        P("segment", None, None),
        P("expert", None),
        P("expert", None),
        P("expert", None),
        P(),
        P(("segment", "expert"), None, None),
        P(("segment", "expert"), None, None),
    )
    out_specs = (P("segment", "expert", None), P("expert", "segment"))
    return jax.shard_map(
        per_device, mesh=mesh, in_specs=in_specs, out_specs=out_specs, check_vma=False
    )
```

```python
import functools
import math

import jax
import jax.numpy as jnp
from jax import lax
from jax.experimental import pallas as pl
from jax.experimental.pallas import tpu as pltpu
from jax.sharding import PartitionSpec as P

LANES = 128
VMEM_BUDGET = 24 << 20
MESH = pl.DeviceIdType.MESH


def grid_sides(count):
    outer = 1
    while outer**3 < count:
        outer *= 2
    rest = count // outer
    middle = 1
    while middle**2 < rest:
        middle *= 2
    return outer, middle, rest // middle


def return_kernel(sides, chunks, act, w_out, wts, out, mine, give, got, *rest):
    n_a, n_b, n_c = sides
    bufs, sems = rest[:12], rest[12:]
    seg = lax.axis_index("segment")
    me = lax.axis_index("expert")
    a, b, c = me // (n_b * n_c), (me // n_c) % n_b, me % n_c
    blocks = n_a * n_b * n_c
    slot_rows = mine.shape[1]
    cap = slot_rows // blocks
    wide = mine.shape[2]
    half = wide // 2
    tile = math.gcd(slot_rows, 256)

    def at(na, nb, nc):
        return (seg, (na * n_b + nb) * n_c + nc)

    partner = (1 - seg, me)

    def peer_a(k):
        return at((a + k) % n_a, b, c)

    def peer_b(k):
        return at(a, (b + k) % n_b, c)

    def peer_c(k):
        return at(a, b, (c + k) % n_c)

    barrier = pltpu.get_barrier_semaphore()
    friends = [partner]
    friends += [peer_a(k) for k in range(1, n_a)]
    friends += [peer_b(k) for k in range(1, n_b)]
    friends += [peer_c(k) for k in range(1, n_c)]
    for friend in friends:
        pl.semaphore_signal(barrier, inc=1, device_id=friend, device_id_type=MESH)
    pl.semaphore_wait(barrier, len(friends))

    orders = (
        ((c, n_c, peer_c), (b, n_b, peer_b)),
        ((b, n_b, peer_b), (c, n_c, peer_c)),
    )

    def swap(j):
        return pltpu.make_async_remote_copy(
            src_ref=give.at[j % 2],
            dst_ref=got.at[j],
            send_sem=sems[0].at[j % 2],
            recv_sem=sems[1].at[j],
            device_id=partner,
            device_id_type=MESH,
        )

    def sends(half_index, phase, j):
        first, second = orders[half_index]
        src, dst = bufs[half_index * 6 + phase * 2 : half_index * 6 + phase * 2 + 2]
        send, recv = sems[2 + half_index * 6 + phase * 2 : 4 + half_index * 6 + phase * 2]
        place, side, peer = (first, second, (a, n_a, peer_a))[phase]
        return [
            pltpu.make_async_remote_copy(
                src_ref=src.at[j % 2, (place + k) % side],
                dst_ref=dst.at[j, k - 1],
                send_sem=send.at[j % 2, k - 1],
                recv_sem=recv.at[j, k - 1],
                device_id=peer(k),
                device_id_type=MESH,
            )
            for k in range(1, side)
        ]

    def project(j):
        columns = pl.ds(pl.multiple_of(j * wide, wide), wide)

        def one(r, dest, base):
            rows = pl.ds(pl.multiple_of(r * tile, tile), tile)
            source = pl.ds(pl.multiple_of(base + r * tile, tile), tile)
            dest[j % 2, rows, :] = jnp.dot(
                act[source, :], w_out[:, columns], preferred_element_type=jnp.float32
            ).astype(jnp.bfloat16)

        @pl.loop(0, slot_rows // tile)
        def _(r):
            one(r, give, 0)

        swap(j).start()

        @pl.loop(0, slot_rows // tile)
        def _(r):
            one(r, mine, slot_rows)

    def spread(j):
        swap(j).wait()

        @pl.loop(0, blocks)
        def _(d):
            da, db, dc = d // (n_b * n_c), (d // n_c) % n_b, d % n_c
            rows = pl.ds(pl.multiple_of(d * cap, cap), cap)
            both = jnp.concatenate([mine[j % 2, rows, :], got[j, rows, :]], axis=0)
            part = jnp.dot(wts[d], both, preferred_element_type=jnp.float32)
            part = part.astype(jnp.bfloat16)
            bufs[0][j % 2, dc, db * n_a + da] = part[:, :half]
            bufs[6][j % 2, db, dc * n_a + da] = part[:, half:]

        for half_index in range(2):
            for copy in sends(half_index, 0, j):
                copy.start()

    def first_sum(j):
        for half_index in range(2):
            (place, side, _), (_, side2, _) = orders[half_index]
            src, dst, nxt = bufs[half_index * 6 : half_index * 6 + 3]
            for copy in sends(half_index, 0, j):
                copy.wait()

            @pl.loop(0, side2 * n_a)
            def _(d):
                total = src[j % 2, place, d].astype(jnp.float32)
                for k in range(side - 1):
                    total += dst[j, k, d].astype(jnp.float32)
                nxt[j % 2, d // n_a, d % n_a] = total.astype(jnp.bfloat16)

            for copy in sends(half_index, 1, j):
                copy.start()

    def second_sum(j):
        for half_index in range(2):
            place, side, _ = orders[half_index][1]
            src, dst, nxt = bufs[half_index * 6 + 2 : half_index * 6 + 5]
            for copy in sends(half_index, 1, j):
                copy.wait()

            @pl.loop(0, n_a)
            def _(d):
                total = src[j % 2, place, d].astype(jnp.float32)
                for k in range(side - 1):
                    total += dst[j, k, d].astype(jnp.float32)
                nxt[j % 2, d] = total.astype(jnp.bfloat16)

            for copy in sends(half_index, 2, j):
                copy.start()

    def last_sum(j):
        for half_index in range(2):
            src, dst = bufs[half_index * 6 + 4 : half_index * 6 + 6]
            for copy in sends(half_index, 2, j):
                copy.wait()
            total = src[j % 2, a].astype(jnp.float32)
            for k in range(n_a - 1):
                total += dst[j, k].astype(jnp.float32)
            columns = pl.ds(pl.multiple_of(j * wide + half_index * half, half), half)
            out[:, columns] = total

    stages = (project, spread, first_sum, second_sum, last_sum)

    @pl.loop(0, chunks + len(stages) - 1)
    def _(step):
        for lag, stage in enumerate(stages):

            @pl.when((step >= lag) & (step - lag < chunks))
            def _():
                stage(step - lag)


def return_call(sides, act, w_out, wts):
    n_a, n_b, n_c = sides
    tok_rows = wts.shape[1]
    slot_rows = act.shape[0] // 2
    half, wide = LANES, 2 * LANES
    block_bytes = tok_rows * half * 2
    chunk_bytes = slot_rows * wide * 2
    for first, second in ((n_c, n_b), (n_b, n_c)):
        chunk_bytes += block_bytes * n_a * (second * (first - 1) + second - 1)
        chunk_bytes += block_bytes * (n_a - 1)
    chunks = w_out.shape[1] // wide
    while chunks % 2 == 0 and chunks * chunk_bytes > VMEM_BUDGET:
        chunks //= 2

    def bf(*shape):
        return pltpu.VMEM(shape, jnp.bfloat16)

    def dma(*shape):
        return pltpu.SemaphoreType.DMA(shape)

    scratch = [bf(2, slot_rows, wide), bf(2, slot_rows, wide), bf(chunks, slot_rows, wide)]
    sems = [dma(2), dma(chunks)]
    for first, second in ((n_c, n_b), (n_b, n_c)):
        scratch += [
            bf(2, first, second * n_a, tok_rows, half),
            bf(chunks, first - 1, second * n_a, tok_rows, half),
            bf(2, second, n_a, tok_rows, half),
            bf(chunks, second - 1, n_a, tok_rows, half),
            bf(2, n_a, tok_rows, half),
            bf(chunks, n_a - 1, tok_rows, half),
        ]
        for side in (first, second, n_a):
            sems += [dma(2, side - 1), dma(chunks, side - 1)]
    piece = chunks * wide
    call = pl.pallas_call(
        functools.partial(return_kernel, sides, chunks),
        out_shape=jax.ShapeDtypeStruct((tok_rows, piece), jnp.float32),
        in_specs=[pl.BlockSpec(memory_space=pltpu.VMEM)] * 3,
        out_specs=pl.BlockSpec(memory_space=pltpu.VMEM),
        scratch_shapes=scratch + sems,
        compiler_params=pltpu.CompilerParams(
            collective_id=0, has_side_effects=True, vmem_limit_bytes=60 * 1024 * 1024
        ),
        name="return_sum",
    )
    parts = [
        call(act, w_out[:, start : start + piece], wts)
        for start in range(0, w_out.shape[1], piece)
    ]
    return parts[0] if len(parts) == 1 else jnp.concatenate(parts, axis=1)


def gather_kernel(sides, chunks, x, info, gains, w_in, act, info_out, *rest):
    (g_a, g_b, info_got, picks, scale, give, mine, got, hid, w_buf) = rest[:10]
    sems = rest[10:]
    n_a, n_b, n_c = sides
    blocks = n_a * n_b * n_c
    seg = lax.axis_index("segment")
    me = lax.axis_index("expert")
    a, b, c = me // (n_b * n_c), (me // n_c) % n_b, me % n_c
    tok_rows, half = x.shape
    part = tok_rows // 2
    wide = half // chunks
    slot_rows = mine.shape[1]
    cap = slot_rows // blocks
    tile = math.gcd(slot_rows, 256)
    units = act.shape[1]
    partner = (1 - seg, me)

    def at(na, nb, nc):
        return (seg, (na * n_b + nb) * n_c + nc)

    def peer_a(k):
        return at((a + k) % n_a, b, c)

    def peer_b(k):
        return at(a, (b + k) % n_b, c)

    def peer_c(k):
        return at(a, b, (c + k) % n_c)

    barrier = pltpu.get_barrier_semaphore()
    pl.semaphore_signal(barrier, inc=1, device_id=partner, device_id_type=MESH)

    @pl.loop(1, blocks)
    def _(k):
        pl.semaphore_signal(
            barrier, inc=1, device_id=(seg, (me + k) % blocks), device_id_type=MESH
        )

    pl.semaphore_wait(barrier, blocks)

    def remote(src, dst, send, recv, peer):
        return pltpu.make_async_remote_copy(
            src_ref=src,
            dst_ref=dst,
            send_sem=send,
            recv_sem=recv,
            device_id=peer,
            device_id_type=MESH,
        )

    def tell(k):
        to = (me + k) % blocks
        return remote(
            info.at[to], info_got.at[me], sems[0].at[k - 1], sems[1].at[k - 1], (seg, to)
        )

    def swap(j):
        return remote(give.at[j % 2], got.at[j], sems[2].at[j % 2], sems[3].at[j], partner)

    orders = (
        (g_a, c, b, n_c, n_b, peer_c, peer_b),
        (g_b, b, c, n_b, n_c, peer_b, peer_c),
    )

    def columns(j):
        return pl.ds(pl.multiple_of(j * wide, wide), wide)

    def sends(which, phase, j):
        held, outer, inner, n_outer, n_inner, peer_outer, peer_inner = orders[which]
        send, recv = sems[5 + which * 6 + phase * 2 : 7 + which * 6 + phase * 2]
        if phase == 0:
            src = x.at[pl.ds(which * part, part), columns(j)]
            dst, side, peer = held.at[j, outer, inner, a], n_a, peer_a
        elif phase == 1:
            src = dst = held.at[j, outer, inner]
            side, peer = n_inner, peer_inner
        else:
            src = dst = held.at[j, outer]
            side, peer = n_outer, peer_outer
        return [
            remote(src, dst, send.at[j % 2, k - 1], recv.at[j, k - 1], peer(k))
            for k in range(1, side)
        ]

    def weight_copies(j):
        copies = []
        for which, owner in enumerate((seg, 1 - seg)):
            rows = pl.ds(pl.multiple_of(owner * half + j * wide, wide), wide)
            copies.append(
                pltpu.make_async_copy(
                    w_in.at[rows, :],
                    w_buf.at[j % 2, pl.ds(which * wide, wide)],
                    sems[4].at[j % 2, which],
                )
            )
        return copies

    def first_send(j):
        for which in range(2):
            held, outer, inner = orders[which][:3]
            for copy in sends(which, 0, j):
                copy.start()
            held[j, outer, inner, a] = x[pl.ds(which * part, part), columns(j)]

    def relay(phase, j):
        for which in range(2):
            for copy in sends(which, phase - 1, j):
                copy.wait()
            for copy in sends(which, phase, j):
                copy.start()

    def read_info():
        info_got[me] = info[me]

        @pl.loop(1, blocks)
        def _(k):
            tell(k).wait()

        row = lax.broadcasted_iota(jnp.int32, (cap, tok_rows), 0).astype(jnp.float32)

        @pl.loop(0, blocks)
        def _(d):
            told = info_got[d]
            info_out[d] = told
            own = told[0:1, :] == row
            other = told[1:2, :] == row
            picks[d] = jnp.concatenate(
                [jnp.where(own, 1.0, 0.0), jnp.where(other, 1.0, 0.0)], axis=0
            ).astype(jnp.bfloat16)
            factor = jnp.sum(jnp.where(own, told[4:5, :], 0.0), axis=1, keepdims=True)
            rows = pl.ds(pl.multiple_of(d * cap, cap), cap)
            scale[rows, :] = jnp.broadcast_to(factor, (cap, wide))

    def pick(j):
        for copy in weight_copies(j):
            copy.start()
        for which in range(2):
            for copy in sends(which, 2, j):
                copy.wait()

        @pl.when(j == 0)
        def _():
            read_info()

        @pl.loop(0, blocks, unroll=4)
        def _(d):
            da, db, dc = d // (n_b * n_c), (d // n_c) % n_b, d % n_c
            rows = pl.ds(pl.multiple_of(d * cap, cap), cap)
            there = jnp.concatenate([g_a[j, dc, db, da], g_b[j, db, dc, da]], axis=0)
            taken = jnp.dot(picks[d], there, preferred_element_type=jnp.float32)
            taken = taken.astype(jnp.bfloat16)
            mine[j % 2, rows, :] = taken[:cap]
            give[j % 2, rows, :] = taken[cap:]

        swap(j).start()

    def multiply(j):
        swap(j).wait()
        for copy in weight_copies(j):
            copy.wait()
        places = [
            pl.ds(pl.multiple_of(owner * half + j * wide, wide), wide) for owner in (seg, 1 - seg)
        ]

        @pl.loop(0, slot_rows // tile)
        def _(r):
            rows = pl.ds(pl.multiple_of(r * tile, tile), tile)
            factor = scale[rows, :]
            pieces = [
                ref[rows, :].astype(jnp.float32) * factor for ref in (mine.at[j % 2], got.at[j])
            ]
            for section in range(2):
                normed = jnp.concatenate(
                    [
                        (piece * gains[pl.ds(section, 1), place]).astype(jnp.bfloat16)
                        for piece, place in zip(pieces, places)
                    ],
                    axis=1,
                )
                to = pl.ds(pl.multiple_of(section * slot_rows + r * tile, tile), tile)
                hid[to, :] += jnp.dot(
                    normed, w_buf[j % 2], preferred_element_type=jnp.float32
                )

    @pl.loop(1, blocks)
    def _(k):
        tell(k).start()

    stages = (
        first_send,
        functools.partial(relay, 1),
        functools.partial(relay, 2),
        pick,
        multiply,
    )

    @pl.loop(0, chunks + len(stages) - 1)
    def _(step):
        for lag, stage in enumerate(stages):

            @pl.when((step >= lag) & (step - lag < chunks))
            def _():
                stage(step - lag)

        @pl.when(step == 0)
        def _():
            @pl.loop(0, 2 * slot_rows // tile)
            def _(r):
                rows = pl.ds(pl.multiple_of(r * tile, tile), tile)
                hid[rows, :] = jnp.zeros((tile, 2 * units), jnp.float32)

    @pl.loop(0, 2 * slot_rows // tile)
    def _(r):
        rows = pl.ds(pl.multiple_of(r * tile, tile), tile)
        gate = hid[rows, :units]
        act[rows, :] = (gate / (1.0 + jnp.exp(-gate)) * hid[rows, units:]).astype(jnp.bfloat16)


def gather_call(sides, room, x, info, gains, w_in):
    n_a, n_b, n_c = sides
    blocks = n_a * n_b * n_c
    tok_rows, half = x.shape
    wide = LANES
    chunks = half // wide
    slot_rows = blocks * room
    units = w_in.shape[1] // 2
    part = tok_rows // 2

    def bf(*shape):
        return pltpu.VMEM(shape, jnp.bfloat16)

    def f32(*shape):
        return pltpu.VMEM(shape, jnp.float32)

    def dma(*shape):
        return pltpu.SemaphoreType.DMA(shape)

    scratch = [
        bf(chunks, n_c, n_b, n_a, part, wide),
        bf(chunks, n_b, n_c, n_a, part, wide),
        f32(*info.shape),
        bf(blocks, 2 * room, tok_rows),
        f32(slot_rows, wide),
        bf(2, slot_rows, wide),
        bf(2, slot_rows, wide),
        bf(chunks, slot_rows, wide),
        f32(2 * slot_rows, 2 * units),
        bf(2, 2 * wide, 2 * units),
    ]
    sems = [dma(blocks - 1), dma(blocks - 1), dma(2), dma(chunks), dma(2, 2)]
    for outer, inner in ((n_c, n_b), (n_b, n_c)):
        for side in (n_a, inner, outer):
            sems += [dma(2, side - 1), dma(chunks, side - 1)]
    vmem = pl.BlockSpec(memory_space=pltpu.VMEM)
    return pl.pallas_call(
        functools.partial(gather_kernel, sides, chunks),
        out_shape=(
            jax.ShapeDtypeStruct((2 * slot_rows, units), jnp.bfloat16),
            jax.ShapeDtypeStruct(info.shape, jnp.float32),
        ),
        in_specs=[vmem, vmem, vmem, pl.BlockSpec(memory_space=pl.ANY)],
        out_specs=(vmem, vmem),
        scratch_shapes=scratch + sems,
        compiler_params=pltpu.CompilerParams(
            collective_id=1, has_side_effects=True, vmem_limit_bytes=60 * 1024 * 1024
        ),
        name="gather_hidden",
    )(x, info, gains, w_in)


def swap_cores(x):
    count = lax.axis_size("segment")
    return lax.ppermute(x, "segment", [(i, count - 1 - i) for i in range(count)])


def inverse_rms(values):
    return lax.rsqrt(jnp.mean(values * values, axis=-1, keepdims=True) + 1e-06)


def per_device(
    rollout,
    norm_gain,
    router_first,
    gain_second,
    router_second,
    expert_ids,
    copy_pick,
    later_ids,
    slot_table,
    expert_in,
    expert_out,
):
    position = lax.axis_index("segment")
    segment_count = lax.axis_size("segment")
    chip_count = lax.axis_size("expert")
    tok_rows, half = rollout.shape
    top_count = expert_ids.shape[1]
    experts_all = router_first.shape[2]
    slot_count = slot_table.shape[0]
    capacity = 3 * tok_rows * top_count // (2 * segment_count * chip_count)

    expert_cols = jnp.arange(experts_all, dtype=jnp.int32)
    slot_ids = jnp.arange(slot_count, dtype=jnp.int32)
    same = slot_table[:, None] == slot_table[None, :]
    earlier = slot_ids[:, None] < slot_ids[None, :]
    copy_rank = jnp.sum((same & earlier).astype(jnp.int32), axis=0)
    slot_holders = jnp.sum(same.astype(jnp.int32), axis=0)
    here = slot_table == expert_ids[..., None]
    copies = jnp.max(jnp.where(here, slot_holders, 1), axis=-1)
    wanted = copy_pick % copies
    match = here & (copy_rank == wanted[..., None])
    hit = jnp.sum(match.astype(jnp.bfloat16), axis=1)
    order = jnp.arange(tok_rows, dtype=jnp.int32)
    before_mask = (order[None, :] < order[:, None]).astype(jnp.bfloat16)
    before = jnp.dot(before_mask, hit, preferred_element_type=jnp.float32).astype(jnp.int32)
    other_half = swap_cores(rollout)
    first = position == 0
    left = jnp.where(first, rollout, other_half)
    right = jnp.where(first, other_half, rollout)
    whole = jnp.concatenate([left, right], axis=1)
    states_in = whole.astype(jnp.float32)
    factor = inverse_rms(states_in)
    normed = (states_in * factor * norm_gain[0].astype(jnp.float32)).astype(
        jnp.bfloat16
    )
    logits = jnp.dot(normed, router_first[0], preferred_element_type=jnp.float32)
    picked = expert_ids[..., None] == expert_cols
    chosen = jnp.sum(jnp.where(picked, logits[:, None, :], 0.0), axis=-1)
    lifted = jnp.exp(chosen - jnp.max(chosen, axis=1, keepdims=True))
    gates = (lifted / jnp.sum(lifted, axis=1, keepdims=True)).astype(jnp.bfloat16)
    place = jnp.where((hit > 0) & (before < capacity), before, -1).astype(jnp.float32)
    gate = jnp.sum(jnp.where(match, gates.astype(jnp.float32)[..., None], 0.0), axis=1)

    def by_core(values):
        cores = values.T.reshape(segment_count, chip_count, tok_rows)
        own = jnp.where(first, cores[0], cores[1])
        other = jnp.where(first, cores[1], cores[0])
        return [own, other]

    factors = jnp.broadcast_to(factor[:, 0], (chip_count, tok_rows))
    blank = jnp.zeros((chip_count, tok_rows), jnp.float32)
    info = jnp.stack(by_core(place) + by_core(gate) + [factors, blank, blank, blank], axis=1)
    gains = jnp.concatenate([swap_cores(norm_gain), norm_gain], axis=0).astype(jnp.float32)
    room = -(-capacity // 16) * 16
    sides = grid_sides(chip_count)
    active, told = gather_call(sides, room, rollout, info, gains, expert_in[0])
    rows = jnp.arange(room, dtype=jnp.float32)

    def spread(place, weight):
        return jnp.where(place[..., None] == rows, weight[..., None], 0.0).astype(jnp.bfloat16)

    weights = jnp.concatenate(
        [spread(told[:, 0], told[:, 2]), spread(told[:, 1], told[:, 3])], axis=2
    )
    summed = return_call(sides, active, expert_out[0], weights)
    mixed = states_in + summed
    later = (mixed * inverse_rms(mixed) * gain_second[0].astype(jnp.float32)).astype(jnp.bfloat16)
    logp = jax.nn.log_softmax(
        jnp.dot(later, router_second[0], preferred_element_type=jnp.float32), axis=-1
    )
    later_pick = later_ids[..., None] == expert_cols
    score = jnp.sum(jnp.where(later_pick, logp[:, None, :], 0.0), axis=(1, 2))
    partner = swap_cores(score)
    ratio = jnp.where(position == 1, score - partner, partner - score)
    paired = ratio.reshape(tok_rows // 2, 2)
    column = lax.dynamic_slice_in_dim(paired, position, 1, 1)
    return (mixed.astype(jnp.bfloat16)[None], column)


def solution(mesh):
    in_specs = (
        P("expert", "segment"),
        P("segment", None),
        P("segment", None, None),
        P("segment", None),
        P("segment", None, None),
        P("expert", None),
        P("expert", None),
        P("expert", None),
        P(),
        P(("segment", "expert"), None, None),
        P(("segment", "expert"), None, None),
    )
    out_specs = (P("segment", "expert", None), P("expert", "segment"))
    return jax.shard_map(
        per_device, mesh=mesh, in_specs=in_specs, out_specs=out_specs, check_vma=False
    )
```

```python
import functools
import math

import jax
import jax.numpy as jnp
from jax import lax
from jax.experimental import pallas as pl
from jax.experimental.pallas import tpu as pltpu
from jax.sharding import PartitionSpec as P

LANES = 128
VMEM_BUDGET = 24 << 20
MESH = pl.DeviceIdType.MESH


def grid_sides(count):
    outer = 1
    while outer**3 < count:
        outer *= 2
    rest = count // outer
    middle = 1
    while middle**2 < rest:
        middle *= 2
    return outer, middle, rest // middle


def return_kernel(sides, chunks, act, w_out, wts, out, mine, give, got, *rest):
    n_a, n_b, n_c = sides
    bufs, sems = rest[:12], rest[12:]
    part = out.shape[0] // 2
    seg = lax.axis_index("segment")
    me = lax.axis_index("expert")
    a, b, c = me // (n_b * n_c), (me // n_c) % n_b, me % n_c
    blocks = n_a * n_b * n_c
    slot_rows = mine.shape[1]
    cap = slot_rows // blocks
    wide = mine.shape[2]
    half = wide // 2
    tile = math.gcd(slot_rows, 256)

    def at(na, nb, nc):
        return (seg, (na * n_b + nb) * n_c + nc)

    partner = (1 - seg, me)

    def peer_a(k):
        return at((a + k) % n_a, b, c)

    def peer_b(k):
        return at(a, (b + k) % n_b, c)

    def peer_c(k):
        return at(a, b, (c + k) % n_c)

    barrier = pltpu.get_barrier_semaphore()
    friends = [partner]
    friends += [peer_a(k) for k in range(1, n_a)]
    friends += [peer_b(k) for k in range(1, n_b)]
    friends += [peer_c(k) for k in range(1, n_c)]
    for friend in friends:
        pl.semaphore_signal(barrier, inc=1, device_id=friend, device_id_type=MESH)
    pl.semaphore_wait(barrier, len(friends))

    orders = (
        ((c, n_c, peer_c), (b, n_b, peer_b)),
        ((b, n_b, peer_b), (c, n_c, peer_c)),
    )

    def swap(j):
        return pltpu.make_async_remote_copy(
            src_ref=give.at[j % 2],
            dst_ref=got.at[j],
            send_sem=sems[0].at[j % 2],
            recv_sem=sems[1].at[j],
            device_id=partner,
            device_id_type=MESH,
        )

    def sends(half_index, phase, j):
        first, second = orders[half_index]
        src, dst = bufs[half_index * 6 + phase * 2 : half_index * 6 + phase * 2 + 2]
        send, recv = sems[2 + half_index * 6 + phase * 2 : 4 + half_index * 6 + phase * 2]
        place, side, peer = (first, second, (a, n_a, peer_a))[phase]
        return [
            pltpu.make_async_remote_copy(
                src_ref=src.at[j % 2, (place + k) % side],
                dst_ref=dst.at[j, k - 1],
                send_sem=send.at[j % 2, k - 1],
                recv_sem=recv.at[j, k - 1],
                device_id=peer(k),
                device_id_type=MESH,
            )
            for k in range(1, side)
        ]

    def project(j):
        columns = pl.ds(pl.multiple_of(j * wide, wide), wide)

        def one(r, dest, base):
            rows = pl.ds(pl.multiple_of(r * tile, tile), tile)
            source = pl.ds(pl.multiple_of(base + r * tile, tile), tile)
            dest[j % 2, rows, :] = jnp.dot(
                act[source, :], w_out[:, columns], preferred_element_type=jnp.float32
            ).astype(jnp.bfloat16)

        @pl.loop(0, slot_rows // tile)
        def _(r):
            one(r, give, 0)

        swap(j).start()

        @pl.loop(0, slot_rows // tile)
        def _(r):
            one(r, mine, slot_rows)

    def spread(j):
        column, turn = j // 2, j % 2

        @pl.when(turn == 0)
        def _():
            swap(column).wait()

        @pl.loop(0, blocks, unroll=4)
        def _(d):
            da, db, dc = d // (n_b * n_c), (d // n_c) % n_b, d % n_c
            rows = pl.ds(pl.multiple_of(d * cap, cap), cap)
            both = jnp.concatenate([mine[column % 2, rows, :], got[column, rows, :]], axis=0)
            given = jnp.dot(wts[turn, d], both, preferred_element_type=jnp.float32)
            given = given.astype(jnp.bfloat16)
            bufs[0][j % 2, dc, db * n_a + da] = given[:, :half]
            bufs[6][j % 2, db, dc * n_a + da] = given[:, half:]

        for half_index in range(2):
            for copy in sends(half_index, 0, j):
                copy.start()

    def first_sum(j):
        for half_index in range(2):
            (place, side, _), (_, side2, _) = orders[half_index]
            src, dst, nxt = bufs[half_index * 6 : half_index * 6 + 3]
            for copy in sends(half_index, 0, j):
                copy.wait()

            @pl.loop(0, side2 * n_a)
            def _(d):
                total = src[j % 2, place, d].astype(jnp.float32)
                for k in range(side - 1):
                    total += dst[j, k, d].astype(jnp.float32)
                nxt[j % 2, d // n_a, d % n_a] = total.astype(jnp.bfloat16)

            for copy in sends(half_index, 1, j):
                copy.start()

    def second_sum(j):
        for half_index in range(2):
            place, side, _ = orders[half_index][1]
            src, dst, nxt = bufs[half_index * 6 + 2 : half_index * 6 + 5]
            for copy in sends(half_index, 1, j):
                copy.wait()

            @pl.loop(0, n_a)
            def _(d):
                total = src[j % 2, place, d].astype(jnp.float32)
                for k in range(side - 1):
                    total += dst[j, k, d].astype(jnp.float32)
                nxt[j % 2, d] = total.astype(jnp.bfloat16)

            for copy in sends(half_index, 2, j):
                copy.start()

    def last_sum(j):
        for half_index in range(2):
            src, dst = bufs[half_index * 6 + 4 : half_index * 6 + 6]
            for copy in sends(half_index, 2, j):
                copy.wait()
            total = src[j % 2, a].astype(jnp.float32)
            for k in range(n_a - 1):
                total += dst[j, k].astype(jnp.float32)
            columns = pl.ds(pl.multiple_of(j // 2 * wide + half_index * half, half), half)
            out[pl.ds(pl.multiple_of(j % 2 * part, part), part), columns] = total

    stages = (
        lambda j: pl.when(j % 2 == 0)(lambda: project(j // 2)),
        spread,
        first_sum,
        second_sum,
        last_sum,
    )

    @pl.loop(0, 2 * chunks + len(stages) - 1)
    def _(step):
        for lag, stage in enumerate(stages):

            @pl.when((step >= lag) & (step - lag < 2 * chunks))
            def _():
                stage(step - lag)


def return_call(sides, act, w_out, wts):
    n_a, n_b, n_c = sides
    part = wts.shape[2]
    tok_rows = 2 * part
    slot_rows = act.shape[0] // 2
    half, wide = LANES, 2 * LANES
    block_bytes = tok_rows * half * 2
    chunk_bytes = slot_rows * wide * 2
    for first, second in ((n_c, n_b), (n_b, n_c)):
        chunk_bytes += block_bytes * n_a * (second * (first - 1) + second - 1)
        chunk_bytes += block_bytes * (n_a - 1)
    chunks = w_out.shape[1] // wide
    while chunks % 2 == 0 and chunks * chunk_bytes > VMEM_BUDGET:
        chunks //= 2

    def bf(*shape):
        return pltpu.VMEM(shape, jnp.bfloat16)

    def dma(*shape):
        return pltpu.SemaphoreType.DMA(shape)

    scratch = [bf(2, slot_rows, wide), bf(2, slot_rows, wide), bf(chunks, slot_rows, wide)]
    sems = [dma(2), dma(chunks)]
    for first, second in ((n_c, n_b), (n_b, n_c)):
        scratch += [
            bf(2, first, second * n_a, part, half),
            bf(2 * chunks, first - 1, second * n_a, part, half),
            bf(2, second, n_a, part, half),
            bf(2 * chunks, second - 1, n_a, part, half),
            bf(2, n_a, part, half),
            bf(2 * chunks, n_a - 1, part, half),
        ]
        for side in (first, second, n_a):
            sems += [dma(2, side - 1), dma(2 * chunks, side - 1)]
    piece = chunks * wide
    call = pl.pallas_call(
        functools.partial(return_kernel, sides, chunks),
        out_shape=jax.ShapeDtypeStruct((tok_rows, piece), jnp.float32),
        in_specs=[pl.BlockSpec(memory_space=pltpu.VMEM)] * 3,
        out_specs=pl.BlockSpec(memory_space=pltpu.VMEM),
        scratch_shapes=scratch + sems,
        compiler_params=pltpu.CompilerParams(
            collective_id=0, has_side_effects=True, vmem_limit_bytes=60 * 1024 * 1024
        ),
        name="return_sum",
    )
    parts = [
        call(act, w_out[:, start : start + piece], wts)
        for start in range(0, w_out.shape[1], piece)
    ]
    return parts[0] if len(parts) == 1 else jnp.concatenate(parts, axis=1)


def gather_kernel(sides, chunks, x, info, gains, w_in, act, info_out, *rest):
    (g_a, g_b, info_got, picks, scale, give, mine, got, hid, w_buf) = rest[:10]
    sems = rest[10:]
    n_a, n_b, n_c = sides
    blocks = n_a * n_b * n_c
    seg = lax.axis_index("segment")
    me = lax.axis_index("expert")
    a, b, c = me // (n_b * n_c), (me // n_c) % n_b, me % n_c
    tok_rows, half = x.shape
    part = tok_rows // 2
    wide = half // chunks
    pair = 2 * wide
    slot_rows = mine.shape[1]
    cap = slot_rows // blocks
    tile = math.gcd(slot_rows, 256)
    units = act.shape[1]
    partner = (1 - seg, me)

    def at(na, nb, nc):
        return (seg, (na * n_b + nb) * n_c + nc)

    def peer_a(k):
        return at((a + k) % n_a, b, c)

    def peer_b(k):
        return at(a, (b + k) % n_b, c)

    def peer_c(k):
        return at(a, b, (c + k) % n_c)

    barrier = pltpu.get_barrier_semaphore()
    pl.semaphore_signal(barrier, inc=1, device_id=partner, device_id_type=MESH)

    @pl.loop(1, blocks)
    def _(k):
        pl.semaphore_signal(
            barrier, inc=1, device_id=(seg, (me + k) % blocks), device_id_type=MESH
        )

    pl.semaphore_wait(barrier, blocks)

    def remote(src, dst, send, recv, peer):
        return pltpu.make_async_remote_copy(
            src_ref=src,
            dst_ref=dst,
            send_sem=send,
            recv_sem=recv,
            device_id=peer,
            device_id_type=MESH,
        )

    def tell(k):
        to = (me + k) % blocks
        return remote(
            info.at[to], info_got.at[me], sems[0].at[k - 1], sems[1].at[k - 1], (seg, to)
        )

    def swap(j):
        return remote(give.at[j % 2], got.at[j], sems[2].at[j % 2], sems[3].at[j], partner)

    orders = (
        (g_a, c, b, n_c, n_b, peer_c, peer_b),
        (g_b, b, c, n_b, n_c, peer_b, peer_c),
    )

    def columns(j):
        return pl.ds(pl.multiple_of(j * wide, wide), wide)

    def sends(which, phase, j):
        held, outer, inner, n_outer, n_inner, peer_outer, peer_inner = orders[which]
        send, recv = sems[5 + which * 6 + phase * 2 : 7 + which * 6 + phase * 2]
        if phase == 0:
            src = x.at[pl.ds(which * part, part), columns(j)]
            dst, side, peer = held.at[j, outer, inner, a], n_a, peer_a
        elif phase == 1:
            src = dst = held.at[j, outer, inner]
            side, peer = n_inner, peer_inner
        else:
            src = dst = held.at[j, outer]
            side, peer = n_outer, peer_outer
        return [
            remote(src, dst, send.at[j % 2, k - 1], recv.at[j, k - 1], peer(k))
            for k in range(1, side)
        ]

    def weight_copies(j):
        copies = []
        for which, owner in enumerate((seg, 1 - seg)):
            rows = pl.ds(pl.multiple_of(owner * half + j * pair, pair), pair)
            copies.append(
                pltpu.make_async_copy(
                    w_in.at[rows, :],
                    w_buf.at[j % 2, pl.ds(which * pair, pair)],
                    sems[4].at[j % 2, which],
                )
            )
        return copies

    def first_send(j):
        for which in range(2):
            held, outer, inner = orders[which][:3]
            for copy in sends(which, 0, j):
                copy.start()
            held[j, outer, inner, a] = x[pl.ds(which * part, part), columns(j)]

    def relay(phase, j):
        for which in range(2):
            for copy in sends(which, phase - 1, j):
                copy.wait()
            for copy in sends(which, phase, j):
                copy.start()

    def read_info():
        info_got[me] = info[me]

        @pl.loop(1, blocks)
        def _(k):
            tell(k).wait()

        row = lax.broadcasted_iota(jnp.int32, (cap, tok_rows), 0).astype(jnp.float32)

        @pl.loop(0, blocks)
        def _(d):
            told = info_got[d]
            info_out[d] = told
            own = told[0:1, :] == row
            other = told[1:2, :] == row
            picks[d] = jnp.concatenate(
                [jnp.where(own, 1.0, 0.0), jnp.where(other, 1.0, 0.0)], axis=0
            ).astype(jnp.bfloat16)
            factor = jnp.sum(jnp.where(own, told[4:5, :], 0.0), axis=1, keepdims=True)
            rows = pl.ds(pl.multiple_of(d * cap, cap), cap)
            scale[rows, :] = jnp.broadcast_to(factor, (cap, pair))

    def settle(j):
        for which in range(2):
            for copy in sends(which, 2, j):
                copy.wait()

        @pl.when(j % 2 == 1)
        def _():
            pick(j // 2)

    def pick(j):
        for copy in weight_copies(j):
            copy.start()

        @pl.when(j == 0)
        def _():
            read_info()

        @pl.loop(0, blocks, unroll=4)
        def _(d):
            da, db, dc = d // (n_b * n_c), (d // n_c) % n_b, d % n_c
            rows = pl.ds(pl.multiple_of(d * cap, cap), cap)
            there = jnp.concatenate(
                [
                    jnp.concatenate([g_a[i, dc, db, da], g_b[i, db, dc, da]], axis=0)
                    for i in (2 * j, 2 * j + 1)
                ],
                axis=1,
            )
            taken = jnp.dot(picks[d], there, preferred_element_type=jnp.float32)
            taken = taken.astype(jnp.bfloat16)
            mine[j % 2, rows, :] = taken[:cap]
            give[j % 2, rows, :] = taken[cap:]

        swap(j).start()

    def multiply(j):
        swap(j).wait()
        for copy in weight_copies(j):
            copy.wait()
        places = [
            pl.ds(pl.multiple_of(owner * half + j * pair, pair), pair) for owner in (seg, 1 - seg)
        ]

        @pl.loop(0, slot_rows // tile)
        def _(r):
            rows = pl.ds(pl.multiple_of(r * tile, tile), tile)
            factor = scale[rows, :]
            pieces = [
                ref[rows, :].astype(jnp.float32) * factor for ref in (mine.at[j % 2], got.at[j])
            ]
            for section in range(2):
                normed = jnp.concatenate(
                    [
                        (piece * gains[pl.ds(section, 1), place]).astype(jnp.bfloat16)
                        for piece, place in zip(pieces, places)
                    ],
                    axis=1,
                )
                to = pl.ds(pl.multiple_of(section * slot_rows + r * tile, tile), tile)
                hid[to, :] += jnp.dot(
                    normed, w_buf[j % 2], preferred_element_type=jnp.float32
                )

    @pl.loop(1, blocks)
    def _(k):
        tell(k).start()

    stages = (
        first_send,
        functools.partial(relay, 1),
        functools.partial(relay, 2),
        settle,
        lambda j: pl.when(j % 2 == 1)(lambda: multiply(j // 2)),
    )

    @pl.loop(0, chunks + len(stages) - 1)
    def _(step):
        for lag, stage in enumerate(stages):

            @pl.when((step >= lag) & (step - lag < chunks))
            def _():
                stage(step - lag)

        @pl.when(step == 0)
        def _():
            @pl.loop(0, 2 * slot_rows // tile)
            def _(r):
                rows = pl.ds(pl.multiple_of(r * tile, tile), tile)
                hid[rows, :] = jnp.zeros((tile, 2 * units), jnp.float32)

    @pl.loop(0, 2 * slot_rows // tile)
    def _(r):
        rows = pl.ds(pl.multiple_of(r * tile, tile), tile)
        gate = hid[rows, :units]
        act[rows, :] = (gate / (1.0 + jnp.exp(-gate)) * hid[rows, units:]).astype(jnp.bfloat16)


def gather_call(sides, room, x, info, gains, w_in):
    n_a, n_b, n_c = sides
    blocks = n_a * n_b * n_c
    tok_rows, half = x.shape
    wide = LANES
    chunks = half // wide
    slot_rows = blocks * room
    units = w_in.shape[1] // 2
    part = tok_rows // 2

    def bf(*shape):
        return pltpu.VMEM(shape, jnp.bfloat16)

    def f32(*shape):
        return pltpu.VMEM(shape, jnp.float32)

    def dma(*shape):
        return pltpu.SemaphoreType.DMA(shape)

    scratch = [
        bf(chunks, n_c, n_b, n_a, part, wide),
        bf(chunks, n_b, n_c, n_a, part, wide),
        f32(*info.shape),
        bf(blocks, 2 * room, tok_rows),
        f32(slot_rows, 2 * wide),
        bf(2, slot_rows, 2 * wide),
        bf(2, slot_rows, 2 * wide),
        bf(chunks // 2, slot_rows, 2 * wide),
        f32(2 * slot_rows, 2 * units),
        bf(2, 4 * wide, 2 * units),
    ]
    sems = [dma(blocks - 1), dma(blocks - 1), dma(2), dma(chunks // 2), dma(2, 2)]
    for outer, inner in ((n_c, n_b), (n_b, n_c)):
        for side in (n_a, inner, outer):
            sems += [dma(2, side - 1), dma(chunks, side - 1)]
    vmem = pl.BlockSpec(memory_space=pltpu.VMEM)
    return pl.pallas_call(
        functools.partial(gather_kernel, sides, chunks),
        out_shape=(
            jax.ShapeDtypeStruct((2 * slot_rows, units), jnp.bfloat16),
            jax.ShapeDtypeStruct(info.shape, jnp.float32),
        ),
        in_specs=[vmem, vmem, vmem, pl.BlockSpec(memory_space=pl.ANY)],
        out_specs=(vmem, vmem),
        scratch_shapes=scratch + sems,
        compiler_params=pltpu.CompilerParams(
            collective_id=1, has_side_effects=True, vmem_limit_bytes=60 * 1024 * 1024
        ),
        name="gather_hidden",
    )(x, info, gains, w_in)


def swap_cores(x):
    count = lax.axis_size("segment")
    return lax.ppermute(x, "segment", [(i, count - 1 - i) for i in range(count)])


def inverse_rms(values):
    return lax.rsqrt(jnp.mean(values * values, axis=-1, keepdims=True) + 1e-06)


def per_device(
    rollout,
    norm_gain,
    router_first,
    gain_second,
    router_second,
    expert_ids,
    copy_pick,
    later_ids,
    slot_table,
    expert_in,
    expert_out,
):
    position = lax.axis_index("segment")
    segment_count = lax.axis_size("segment")
    chip_count = lax.axis_size("expert")
    tok_rows, half = rollout.shape
    top_count = expert_ids.shape[1]
    experts_all = router_first.shape[2]
    slot_count = slot_table.shape[0]
    capacity = 3 * tok_rows * top_count // (2 * segment_count * chip_count)

    expert_cols = jnp.arange(experts_all, dtype=jnp.int32)
    slot_ids = jnp.arange(slot_count, dtype=jnp.int32)
    same = slot_table[:, None] == slot_table[None, :]
    earlier = slot_ids[:, None] < slot_ids[None, :]
    copy_rank = jnp.sum((same & earlier).astype(jnp.int32), axis=0)
    slot_holders = jnp.sum(same.astype(jnp.int32), axis=0)
    here = slot_table == expert_ids[..., None]
    copies = jnp.max(jnp.where(here, slot_holders, 1), axis=-1)
    wanted = copy_pick % copies
    match = here & (copy_rank == wanted[..., None])
    hit = jnp.sum(match.astype(jnp.bfloat16), axis=1)
    order = jnp.arange(tok_rows, dtype=jnp.int32)
    before_mask = (order[None, :] < order[:, None]).astype(jnp.bfloat16)
    before = jnp.dot(before_mask, hit, preferred_element_type=jnp.float32).astype(jnp.int32)
    other_half = swap_cores(rollout)
    first = position == 0
    left = jnp.where(first, rollout, other_half)
    right = jnp.where(first, other_half, rollout)
    whole = jnp.concatenate([left, right], axis=1)
    states_in = whole.astype(jnp.float32)
    factor = inverse_rms(states_in)
    normed = (states_in * factor * norm_gain[0].astype(jnp.float32)).astype(
        jnp.bfloat16
    )
    logits = jnp.dot(normed, router_first[0], preferred_element_type=jnp.float32)
    picked = expert_ids[..., None] == expert_cols
    chosen = jnp.sum(jnp.where(picked, logits[:, None, :], 0.0), axis=-1)
    lifted = jnp.exp(chosen - jnp.max(chosen, axis=1, keepdims=True))
    gates = (lifted / jnp.sum(lifted, axis=1, keepdims=True)).astype(jnp.bfloat16)
    place = jnp.where((hit > 0) & (before < capacity), before, -1).astype(jnp.float32)
    gate = jnp.sum(jnp.where(match, gates.astype(jnp.float32)[..., None], 0.0), axis=1)

    def by_core(values):
        cores = values.T.reshape(segment_count, chip_count, tok_rows)
        own = jnp.where(first, cores[0], cores[1])
        other = jnp.where(first, cores[1], cores[0])
        return [own, other]

    factors = jnp.broadcast_to(factor[:, 0], (chip_count, tok_rows))
    blank = jnp.zeros((chip_count, tok_rows), jnp.float32)
    info = jnp.stack(by_core(place) + by_core(gate) + [factors, blank, blank, blank], axis=1)
    gains = jnp.concatenate([swap_cores(norm_gain), norm_gain], axis=0).astype(jnp.float32)
    room = -(-capacity // 16) * 16
    sides = grid_sides(chip_count)
    active, told = gather_call(sides, room, rollout, info, gains, expert_in[0])
    rows = jnp.arange(room, dtype=jnp.float32)

    def spread(place, weight):
        return jnp.where(place[..., None] == rows, weight[..., None], 0.0).astype(jnp.bfloat16)

    weights = jnp.concatenate(
        [spread(told[:, 0], told[:, 2]), spread(told[:, 1], told[:, 3])], axis=2
    )
    weights = weights.reshape(chip_count, 2, tok_rows // 2, 2 * room).transpose(1, 0, 2, 3)
    summed = return_call(sides, active, expert_out[0], weights)
    mixed = states_in + summed
    later = (mixed * inverse_rms(mixed) * gain_second[0].astype(jnp.float32)).astype(jnp.bfloat16)
    logp = jax.nn.log_softmax(
        jnp.dot(later, router_second[0], preferred_element_type=jnp.float32), axis=-1
    )
    later_pick = later_ids[..., None] == expert_cols
    score = jnp.sum(jnp.where(later_pick, logp[:, None, :], 0.0), axis=(1, 2))
    partner = swap_cores(score)
    ratio = jnp.where(position == 1, score - partner, partner - score)
    paired = ratio.reshape(tok_rows // 2, 2)
    column = lax.dynamic_slice_in_dim(paired, position, 1, 1)
    return (mixed.astype(jnp.bfloat16)[None], column)


def solution(mesh):
    in_specs = (
        P("expert", "segment"),
        P("segment", None),
        P("segment", None, None),
        P("segment", None),
        P("segment", None, None),
        P("expert", None),
        P("expert", None),
        P("expert", None),
        P(),
        P(("segment", "expert"), None, None),
        P(("segment", "expert"), None, None),
    )
    out_specs = (P("segment", "expert", None), P("expert", "segment"))
    return jax.shard_map(
        per_device, mesh=mesh, in_specs=in_specs, out_specs=out_specs, check_vma=False
    )
```

```python
import functools
import math

import jax
import jax.numpy as jnp
from jax import lax
from jax.experimental import pallas as pl
from jax.experimental.pallas import tpu as pltpu
from jax.sharding import PartitionSpec as P

LANES = 128
DEPTH = 3
VMEM_BUDGET = 24 << 20
MESH = pl.DeviceIdType.MESH


def grid_sides(count):
    outer = 1
    while outer**3 < count:
        outer *= 2
    rest = count // outer
    middle = 1
    while middle**2 < rest:
        middle *= 2
    return outer, middle, rest // middle


def return_kernel(sides, chunks, act, w_out, wts, out, mine, give, got, *rest):
    n_a, n_b, n_c = sides
    bufs, sems = rest[:12], rest[12:]
    seg = lax.axis_index("segment")
    me = lax.axis_index("expert")
    a, b, c = me // (n_b * n_c), (me // n_c) % n_b, me % n_c
    blocks = n_a * n_b * n_c
    slot_rows = mine.shape[1]
    cap = slot_rows // blocks
    wide = mine.shape[2]
    half = wide // 2
    tile = math.gcd(slot_rows, 256)

    def at(na, nb, nc):
        return (seg, (na * n_b + nb) * n_c + nc)

    partner = (1 - seg, me)

    def peer_a(k):
        return at((a + k) % n_a, b, c)

    def peer_b(k):
        return at(a, (b + k) % n_b, c)

    def peer_c(k):
        return at(a, b, (c + k) % n_c)

    barrier = pltpu.get_barrier_semaphore()
    friends = [partner]
    friends += [peer_a(k) for k in range(1, n_a)]
    friends += [peer_b(k) for k in range(1, n_b)]
    friends += [peer_c(k) for k in range(1, n_c)]
    for friend in friends:
        pl.semaphore_signal(barrier, inc=1, device_id=friend, device_id_type=MESH)
    pl.semaphore_wait(barrier, len(friends))

    orders = (
        ((c, n_c, peer_c), (b, n_b, peer_b)),
        ((b, n_b, peer_b), (c, n_c, peer_c)),
    )

    def swap(j):
        return pltpu.make_async_remote_copy(
            src_ref=give.at[j % 2],
            dst_ref=got.at[j],
            send_sem=sems[0].at[j % 2],
            recv_sem=sems[1].at[j],
            device_id=partner,
            device_id_type=MESH,
        )

    def sends(half_index, phase, j):
        first, second = orders[half_index]
        src, dst = bufs[half_index * 6 + phase * 2 : half_index * 6 + phase * 2 + 2]
        send, recv = sems[2 + half_index * 6 + phase * 2 : 4 + half_index * 6 + phase * 2]
        place, side, peer = (first, second, (a, n_a, peer_a))[phase]
        return [
            pltpu.make_async_remote_copy(
                src_ref=src.at[j % DEPTH, (place + k) % side],
                dst_ref=dst.at[j, k - 1],
                send_sem=send.at[j % DEPTH, k - 1],
                recv_sem=recv.at[j, k - 1],
                device_id=peer(k),
                device_id_type=MESH,
            )
            for k in range(1, side)
        ]

    def project(j):
        columns = pl.ds(pl.multiple_of(j * wide, wide), wide)

        def one(r, dest, base):
            rows = pl.ds(pl.multiple_of(r * tile, tile), tile)
            source = pl.ds(pl.multiple_of(base + r * tile, tile), tile)
            dest[j % 2, rows, :] = jnp.dot(
                act[source, :], w_out[:, columns], preferred_element_type=jnp.float32
            ).astype(jnp.bfloat16)

        @pl.loop(0, slot_rows // tile)
        def _(r):
            one(r, give, 0)

        swap(j).start()

        @pl.loop(0, slot_rows // tile)
        def _(r):
            one(r, mine, slot_rows)

    def spread(j):
        swap(j).wait()

        @pl.loop(0, blocks)
        def _(d):
            da, db, dc = d // (n_b * n_c), (d // n_c) % n_b, d % n_c
            rows = pl.ds(pl.multiple_of(d * cap, cap), cap)
            both = jnp.concatenate([mine[j % 2, rows, :], got[j, rows, :]], axis=0)
            part = jnp.dot(wts[d], both, preferred_element_type=jnp.float32)
            part = part.astype(jnp.bfloat16)
            bufs[0][j % DEPTH, dc, db * n_a + da] = part[:, :half]
            bufs[6][j % DEPTH, db, dc * n_a + da] = part[:, half:]

        for half_index in range(2):
            for copy in sends(half_index, 0, j):
                copy.start()

    def first_sum(j):
        for half_index in range(2):
            (place, side, _), (_, side2, _) = orders[half_index]
            src, dst, nxt = bufs[half_index * 6 : half_index * 6 + 3]
            for copy in sends(half_index, 0, j):
                copy.wait()

            @pl.loop(0, side2 * n_a)
            def _(d):
                total = src[j % DEPTH, place, d].astype(jnp.float32)
                for k in range(side - 1):
                    total += dst[j, k, d].astype(jnp.float32)
                nxt[j % DEPTH, d // n_a, d % n_a] = total.astype(jnp.bfloat16)

            for copy in sends(half_index, 1, j):
                copy.start()

    def second_sum(j):
        for half_index in range(2):
            place, side, _ = orders[half_index][1]
            src, dst, nxt = bufs[half_index * 6 + 2 : half_index * 6 + 5]
            for copy in sends(half_index, 1, j):
                copy.wait()

            @pl.loop(0, n_a)
            def _(d):
                total = src[j % DEPTH, place, d].astype(jnp.float32)
                for k in range(side - 1):
                    total += dst[j, k, d].astype(jnp.float32)
                nxt[j % DEPTH, d] = total.astype(jnp.bfloat16)

            for copy in sends(half_index, 2, j):
                copy.start()

    def last_sum(j):
        for half_index in range(2):
            src, dst = bufs[half_index * 6 + 4 : half_index * 6 + 6]
            for copy in sends(half_index, 2, j):
                copy.wait()
            total = src[j % DEPTH, a].astype(jnp.float32)
            for k in range(n_a - 1):
                total += dst[j, k].astype(jnp.float32)
            columns = pl.ds(pl.multiple_of(j * wide + half_index * half, half), half)
            out[:, columns] = total

    stages = ((0, project), (1, spread), (3, first_sum), (5, second_sum), (7, last_sum))

    @pl.loop(0, chunks + stages[-1][0])
    def _(step):
        for lag, stage in stages:

            @pl.when((step >= lag) & (step - lag < chunks))
            def _():
                stage(step - lag)


def return_call(sides, act, w_out, wts):
    n_a, n_b, n_c = sides
    tok_rows = wts.shape[1]
    slot_rows = act.shape[0] // 2
    half, wide = LANES, 2 * LANES
    block_bytes = tok_rows * half * 2
    chunk_bytes = slot_rows * wide * 2
    for first, second in ((n_c, n_b), (n_b, n_c)):
        chunk_bytes += block_bytes * n_a * (second * (first - 1) + second - 1)
        chunk_bytes += block_bytes * (n_a - 1)
    chunks = w_out.shape[1] // wide
    while chunks % 2 == 0 and chunks * chunk_bytes > VMEM_BUDGET:
        chunks //= 2

    def bf(*shape):
        return pltpu.VMEM(shape, jnp.bfloat16)

    def dma(*shape):
        return pltpu.SemaphoreType.DMA(shape)

    scratch = [bf(2, slot_rows, wide), bf(2, slot_rows, wide), bf(chunks, slot_rows, wide)]
    sems = [dma(2), dma(chunks)]
    for first, second in ((n_c, n_b), (n_b, n_c)):
        scratch += [
            bf(DEPTH, first, second * n_a, tok_rows, half),
            bf(chunks, first - 1, second * n_a, tok_rows, half),
            bf(DEPTH, second, n_a, tok_rows, half),
            bf(chunks, second - 1, n_a, tok_rows, half),
            bf(DEPTH, n_a, tok_rows, half),
            bf(chunks, n_a - 1, tok_rows, half),
        ]
        for side in (first, second, n_a):
            sems += [dma(DEPTH, side - 1), dma(chunks, side - 1)]
    piece = chunks * wide
    call = pl.pallas_call(
        functools.partial(return_kernel, sides, chunks),
        out_shape=jax.ShapeDtypeStruct((tok_rows, piece), jnp.float32),
        in_specs=[pl.BlockSpec(memory_space=pltpu.VMEM)] * 3,
        out_specs=pl.BlockSpec(memory_space=pltpu.VMEM),
        scratch_shapes=scratch + sems,
        compiler_params=pltpu.CompilerParams(
            collective_id=0, has_side_effects=True, vmem_limit_bytes=60 * 1024 * 1024
        ),
        name="return_sum",
    )
    parts = [
        call(act, w_out[:, start : start + piece], wts)
        for start in range(0, w_out.shape[1], piece)
    ]
    return parts[0] if len(parts) == 1 else jnp.concatenate(parts, axis=1)


def gather_kernel(sides, chunks, x, info, gains, w_in, act, info_out, *rest):
    (g_a, g_b, info_got, picks, scale, give, mine, got, hid, w_buf) = rest[:10]
    sems = rest[10:]
    n_a, n_b, n_c = sides
    blocks = n_a * n_b * n_c
    seg = lax.axis_index("segment")
    me = lax.axis_index("expert")
    a, b, c = me // (n_b * n_c), (me // n_c) % n_b, me % n_c
    tok_rows, half = x.shape
    part = tok_rows // 2
    wide = half // chunks
    slot_rows = mine.shape[1]
    cap = slot_rows // blocks
    tile = math.gcd(slot_rows, 256)
    units = act.shape[1]
    partner = (1 - seg, me)

    def at(na, nb, nc):
        return (seg, (na * n_b + nb) * n_c + nc)

    def peer_a(k):
        return at((a + k) % n_a, b, c)

    def peer_b(k):
        return at(a, (b + k) % n_b, c)

    def peer_c(k):
        return at(a, b, (c + k) % n_c)

    barrier = pltpu.get_barrier_semaphore()
    pl.semaphore_signal(barrier, inc=1, device_id=partner, device_id_type=MESH)

    @pl.loop(1, blocks)
    def _(k):
        pl.semaphore_signal(
            barrier, inc=1, device_id=(seg, (me + k) % blocks), device_id_type=MESH
        )

    pl.semaphore_wait(barrier, blocks)

    def remote(src, dst, send, recv, peer):
        return pltpu.make_async_remote_copy(
            src_ref=src,
            dst_ref=dst,
            send_sem=send,
            recv_sem=recv,
            device_id=peer,
            device_id_type=MESH,
        )

    def tell(k):
        to = (me + k) % blocks
        return remote(
            info.at[to], info_got.at[me], sems[0].at[k - 1], sems[1].at[k - 1], (seg, to)
        )

    def swap(j):
        return remote(give.at[j % 2], got.at[j], sems[2].at[j % 2], sems[3].at[j], partner)

    orders = (
        (g_a, c, b, n_c, n_b, peer_c, peer_b),
        (g_b, b, c, n_b, n_c, peer_b, peer_c),
    )

    def columns(j):
        return pl.ds(pl.multiple_of(j * wide, wide), wide)

    def sends(which, phase, j):
        held, outer, inner, n_outer, n_inner, peer_outer, peer_inner = orders[which]
        send, recv = sems[5 + which * 6 + phase * 2 : 7 + which * 6 + phase * 2]
        if phase == 0:
            src = x.at[pl.ds(which * part, part), columns(j)]
            dst, side, peer = held.at[j, outer, inner, a], n_a, peer_a
        elif phase == 1:
            src = dst = held.at[j, outer, inner]
            side, peer = n_inner, peer_inner
        else:
            src = dst = held.at[j, outer]
            side, peer = n_outer, peer_outer
        return [
            remote(src, dst, send.at[j % DEPTH, k - 1], recv.at[j, k - 1], peer(k))
            for k in range(1, side)
        ]

    def weight_copies(j):
        copies = []
        for which, owner in enumerate((seg, 1 - seg)):
            rows = pl.ds(pl.multiple_of(owner * half + j * wide, wide), wide)
            copies.append(
                pltpu.make_async_copy(
                    w_in.at[rows, :],
                    w_buf.at[j % 2, pl.ds(which * wide, wide)],
                    sems[4].at[j % 2, which],
                )
            )
        return copies

    def first_send(j):
        for which in range(2):
            held, outer, inner = orders[which][:3]
            for copy in sends(which, 0, j):
                copy.start()
            held[j, outer, inner, a] = x[pl.ds(which * part, part), columns(j)]

    def relay(phase, j):
        for which in range(2):
            for copy in sends(which, phase - 1, j):
                copy.wait()
            for copy in sends(which, phase, j):
                copy.start()

    def read_info():
        info_got[me] = info[me]

        @pl.loop(1, blocks)
        def _(k):
            tell(k).wait()

        row = lax.broadcasted_iota(jnp.int32, (cap, tok_rows), 0).astype(jnp.float32)

        @pl.loop(0, blocks)
        def _(d):
            told = info_got[d]
            info_out[d] = told
            own = told[0:1, :] == row
            other = told[1:2, :] == row
            picks[d] = jnp.concatenate(
                [jnp.where(own, 1.0, 0.0), jnp.where(other, 1.0, 0.0)], axis=0
            ).astype(jnp.bfloat16)
            factor = jnp.sum(jnp.where(own, told[4:5, :], 0.0), axis=1, keepdims=True)
            rows = pl.ds(pl.multiple_of(d * cap, cap), cap)
            scale[rows, :] = jnp.broadcast_to(factor, (cap, wide))

    def pick(j):
        for copy in weight_copies(j):
            copy.start()
        for which in range(2):
            for copy in sends(which, 2, j):
                copy.wait()

        @pl.when(j == 0)
        def _():
            read_info()

        @pl.loop(0, blocks, unroll=4)
        def _(d):
            da, db, dc = d // (n_b * n_c), (d // n_c) % n_b, d % n_c
            rows = pl.ds(pl.multiple_of(d * cap, cap), cap)
            there = jnp.concatenate([g_a[j, dc, db, da], g_b[j, db, dc, da]], axis=0)
            taken = jnp.dot(picks[d], there, preferred_element_type=jnp.float32)
            taken = taken.astype(jnp.bfloat16)
            mine[j % 2, rows, :] = taken[:cap]
            give[j % 2, rows, :] = taken[cap:]

        swap(j).start()

    def multiply(j):
        swap(j).wait()
        for copy in weight_copies(j):
            copy.wait()
        places = [
            pl.ds(pl.multiple_of(owner * half + j * wide, wide), wide) for owner in (seg, 1 - seg)
        ]

        @pl.loop(0, slot_rows // tile)
        def _(r):
            rows = pl.ds(pl.multiple_of(r * tile, tile), tile)
            factor = scale[rows, :]
            pieces = [
                ref[rows, :].astype(jnp.float32) * factor for ref in (mine.at[j % 2], got.at[j])
            ]
            for section in range(2):
                normed = jnp.concatenate(
                    [
                        (piece * gains[pl.ds(section, 1), place]).astype(jnp.bfloat16)
                        for piece, place in zip(pieces, places)
                    ],
                    axis=1,
                )
                to = pl.ds(pl.multiple_of(section * slot_rows + r * tile, tile), tile)
                hid[to, :] += jnp.dot(
                    normed, w_buf[j % 2], preferred_element_type=jnp.float32
                )

    @pl.loop(1, blocks)
    def _(k):
        tell(k).start()

    stages = (
        (0, first_send),
        (2, functools.partial(relay, 1)),
        (4, functools.partial(relay, 2)),
        (6, pick),
        (7, multiply),
    )

    @pl.loop(0, chunks + stages[-1][0])
    def _(step):
        for lag, stage in stages:

            @pl.when((step >= lag) & (step - lag < chunks))
            def _():
                stage(step - lag)

        @pl.when(step == 0)
        def _():
            @pl.loop(0, 2 * slot_rows // tile)
            def _(r):
                rows = pl.ds(pl.multiple_of(r * tile, tile), tile)
                hid[rows, :] = jnp.zeros((tile, 2 * units), jnp.float32)

    @pl.loop(0, 2 * slot_rows // tile)
    def _(r):
        rows = pl.ds(pl.multiple_of(r * tile, tile), tile)
        gate = hid[rows, :units]
        act[rows, :] = (gate / (1.0 + jnp.exp(-gate)) * hid[rows, units:]).astype(jnp.bfloat16)


def gather_call(sides, room, x, info, gains, w_in):
    n_a, n_b, n_c = sides
    blocks = n_a * n_b * n_c
    tok_rows, half = x.shape
    wide = LANES
    chunks = half // wide
    slot_rows = blocks * room
    units = w_in.shape[1] // 2
    part = tok_rows // 2

    def bf(*shape):
        return pltpu.VMEM(shape, jnp.bfloat16)

    def f32(*shape):
        return pltpu.VMEM(shape, jnp.float32)

    def dma(*shape):
        return pltpu.SemaphoreType.DMA(shape)

    scratch = [
        bf(chunks, n_c, n_b, n_a, part, wide),
        bf(chunks, n_b, n_c, n_a, part, wide),
        f32(*info.shape),
        bf(blocks, 2 * room, tok_rows),
        f32(slot_rows, wide),
        bf(2, slot_rows, wide),
        bf(2, slot_rows, wide),
        bf(chunks, slot_rows, wide),
        f32(2 * slot_rows, 2 * units),
        bf(2, 2 * wide, 2 * units),
    ]
    sems = [dma(blocks - 1), dma(blocks - 1), dma(2), dma(chunks), dma(2, 2)]
    for outer, inner in ((n_c, n_b), (n_b, n_c)):
        for side in (n_a, inner, outer):
            sems += [dma(DEPTH, side - 1), dma(chunks, side - 1)]
    vmem = pl.BlockSpec(memory_space=pltpu.VMEM)
    return pl.pallas_call(
        functools.partial(gather_kernel, sides, chunks),
        out_shape=(
            jax.ShapeDtypeStruct((2 * slot_rows, units), jnp.bfloat16),
            jax.ShapeDtypeStruct(info.shape, jnp.float32),
        ),
        in_specs=[vmem, vmem, vmem, pl.BlockSpec(memory_space=pl.ANY)],
        out_specs=(vmem, vmem),
        scratch_shapes=scratch + sems,
        compiler_params=pltpu.CompilerParams(
            collective_id=1, has_side_effects=True, vmem_limit_bytes=60 * 1024 * 1024
        ),
        name="gather_hidden",
    )(x, info, gains, w_in)


def swap_cores(x):
    count = lax.axis_size("segment")
    return lax.ppermute(x, "segment", [(i, count - 1 - i) for i in range(count)])


def inverse_rms(values):
    return lax.rsqrt(jnp.mean(values * values, axis=-1, keepdims=True) + 1e-06)


def per_device(
    rollout,
    norm_gain,
    router_first,
    gain_second,
    router_second,
    expert_ids,
    copy_pick,
    later_ids,
    slot_table,
    expert_in,
    expert_out,
):
    position = lax.axis_index("segment")
    segment_count = lax.axis_size("segment")
    chip_count = lax.axis_size("expert")
    tok_rows, half = rollout.shape
    top_count = expert_ids.shape[1]
    experts_all = router_first.shape[2]
    slot_count = slot_table.shape[0]
    capacity = 3 * tok_rows * top_count // (2 * segment_count * chip_count)

    expert_cols = jnp.arange(experts_all, dtype=jnp.int32)
    slot_ids = jnp.arange(slot_count, dtype=jnp.int32)
    same = slot_table[:, None] == slot_table[None, :]
    earlier = slot_ids[:, None] < slot_ids[None, :]
    copy_rank = jnp.sum((same & earlier).astype(jnp.int32), axis=0)
    slot_holders = jnp.sum(same.astype(jnp.int32), axis=0)
    here = slot_table == expert_ids[..., None]
    copies = jnp.max(jnp.where(here, slot_holders, 1), axis=-1)
    wanted = copy_pick % copies
    match = here & (copy_rank == wanted[..., None])
    hit = jnp.sum(match.astype(jnp.bfloat16), axis=1)
    order = jnp.arange(tok_rows, dtype=jnp.int32)
    before_mask = (order[None, :] < order[:, None]).astype(jnp.bfloat16)
    before = jnp.dot(before_mask, hit, preferred_element_type=jnp.float32).astype(jnp.int32)
    other_half = swap_cores(rollout)
    first = position == 0
    left = jnp.where(first, rollout, other_half)
    right = jnp.where(first, other_half, rollout)
    whole = jnp.concatenate([left, right], axis=1)
    states_in = whole.astype(jnp.float32)
    factor = inverse_rms(states_in)
    normed = (states_in * factor * norm_gain[0].astype(jnp.float32)).astype(
        jnp.bfloat16
    )
    logits = jnp.dot(normed, router_first[0], preferred_element_type=jnp.float32)
    picked = expert_ids[..., None] == expert_cols
    chosen = jnp.sum(jnp.where(picked, logits[:, None, :], 0.0), axis=-1)
    lifted = jnp.exp(chosen - jnp.max(chosen, axis=1, keepdims=True))
    gates = (lifted / jnp.sum(lifted, axis=1, keepdims=True)).astype(jnp.bfloat16)
    place = jnp.where((hit > 0) & (before < capacity), before, -1).astype(jnp.float32)
    gate = jnp.sum(jnp.where(match, gates.astype(jnp.float32)[..., None], 0.0), axis=1)

    def by_core(values):
        cores = values.T.reshape(segment_count, chip_count, tok_rows)
        own = jnp.where(first, cores[0], cores[1])
        other = jnp.where(first, cores[1], cores[0])
        return [own, other]

    factors = jnp.broadcast_to(factor[:, 0], (chip_count, tok_rows))
    blank = jnp.zeros((chip_count, tok_rows), jnp.float32)
    info = jnp.stack(by_core(place) + by_core(gate) + [factors, blank, blank, blank], axis=1)
    gains = jnp.concatenate([swap_cores(norm_gain), norm_gain], axis=0).astype(jnp.float32)
    room = -(-capacity // 16) * 16
    sides = grid_sides(chip_count)
    active, told = gather_call(sides, room, rollout, info, gains, expert_in[0])
    rows = jnp.arange(room, dtype=jnp.float32)

    def spread(place, weight):
        return jnp.where(place[..., None] == rows, weight[..., None], 0.0).astype(jnp.bfloat16)

    weights = jnp.concatenate(
        [spread(told[:, 0], told[:, 2]), spread(told[:, 1], told[:, 3])], axis=2
    )
    summed = return_call(sides, active, expert_out[0], weights)
    mixed = states_in + summed
    later = (mixed * inverse_rms(mixed) * gain_second[0].astype(jnp.float32)).astype(jnp.bfloat16)
    logp = jax.nn.log_softmax(
        jnp.dot(later, router_second[0], preferred_element_type=jnp.float32), axis=-1
    )
    later_pick = later_ids[..., None] == expert_cols
    score = jnp.sum(jnp.where(later_pick, logp[:, None, :], 0.0), axis=(1, 2))
    partner = swap_cores(score)
    ratio = jnp.where(position == 1, score - partner, partner - score)
    paired = ratio.reshape(tok_rows // 2, 2)
    column = lax.dynamic_slice_in_dim(paired, position, 1, 1)
    return (mixed.astype(jnp.bfloat16)[None], column)


def solution(mesh):
    in_specs = (
        P("expert", "segment"),
        P("segment", None),
        P("segment", None, None),
        P("segment", None),
        P("segment", None, None),
        P("expert", None),
        P("expert", None),
        P("expert", None),
        P(),
        P(("segment", "expert"), None, None),
        P(("segment", "expert"), None, None),
    )
    out_specs = (P("segment", "expert", None), P("expert", "segment"))
    return jax.shard_map(
        per_device, mesh=mesh, in_specs=in_specs, out_specs=out_specs, check_vma=False
    )
```

```python
import functools
import math

import jax
import jax.numpy as jnp
from jax import lax
from jax.experimental import pallas as pl
from jax.experimental.pallas import tpu as pltpu
from jax.sharding import PartitionSpec as P

LANES = 128
VMEM_BUDGET = 24 << 20
MESH = pl.DeviceIdType.MESH


def grid_sides(count):
    outer = 1
    while outer**3 < count:
        outer *= 2
    rest = count // outer
    middle = 1
    while middle**2 < rest:
        middle *= 2
    return outer, middle, rest // middle


def return_kernel(sides, chunks, act, w_out, wts, out, mine, give, got, *rest):
    n_a, n_b, n_c = sides
    bufs, sems = rest[:12], rest[12:]
    seg = lax.axis_index("segment")
    me = lax.axis_index("expert")
    a, b, c = me // (n_b * n_c), (me // n_c) % n_b, me % n_c
    blocks = n_a * n_b * n_c
    slot_rows = mine.shape[1]
    cap = slot_rows // blocks
    wide = mine.shape[2]
    half = wide // 2
    tile = math.gcd(slot_rows, 256)

    def at(na, nb, nc):
        return (seg, (na * n_b + nb) * n_c + nc)

    partner = (1 - seg, me)

    def peer_a(k):
        return at((a + k) % n_a, b, c)

    def peer_b(k):
        return at(a, (b + k) % n_b, c)

    def peer_c(k):
        return at(a, b, (c + k) % n_c)

    barrier = pltpu.get_barrier_semaphore()
    friends = [partner]
    friends += [peer_a(k) for k in range(1, n_a)]
    friends += [peer_b(k) for k in range(1, n_b)]
    friends += [peer_c(k) for k in range(1, n_c)]
    for friend in friends:
        pl.semaphore_signal(barrier, inc=1, device_id=friend, device_id_type=MESH)
    pl.semaphore_wait(barrier, len(friends))

    orders = (
        ((c, n_c, peer_c), (b, n_b, peer_b)),
        ((b, n_b, peer_b), (c, n_c, peer_c)),
    )

    def swap(j):
        return pltpu.make_async_remote_copy(
            src_ref=give.at[j % 2],
            dst_ref=got.at[j],
            send_sem=sems[0].at[j % 2],
            recv_sem=sems[1].at[j],
            device_id=partner,
            device_id_type=MESH,
        )

    def sends(half_index, phase, j):
        first, second = orders[half_index]
        src, dst = bufs[half_index * 6 + phase * 2 : half_index * 6 + phase * 2 + 2]
        send, recv = sems[2 + half_index * 6 + phase * 2 : 4 + half_index * 6 + phase * 2]
        place, side, peer = (first, second, (a, n_a, peer_a))[phase]
        return [
            pltpu.make_async_remote_copy(
                src_ref=src.at[j % 2, (place + k) % side],
                dst_ref=dst.at[j, k - 1],
                send_sem=send.at[j % 2, k - 1],
                recv_sem=recv.at[j, k - 1],
                device_id=peer(k),
                device_id_type=MESH,
            )
            for k in range(1, side)
        ]

    def project(j):
        columns = pl.ds(pl.multiple_of(j * wide, wide), wide)

        def one(r, dest, base):
            rows = pl.ds(pl.multiple_of(r * tile, tile), tile)
            source = pl.ds(pl.multiple_of(base + r * tile, tile), tile)
            dest[j % 2, rows, :] = jnp.dot(
                act[source, :], w_out[:, columns], preferred_element_type=jnp.float32
            ).astype(jnp.bfloat16)

        @pl.loop(0, slot_rows // tile)
        def _(r):
            one(r, give, 0)

        swap(j).start()

        @pl.loop(0, slot_rows // tile)
        def _(r):
            one(r, mine, slot_rows)

    def spread(j):
        swap(j).wait()

        @pl.loop(0, blocks)
        def _(d):
            da, db, dc = d // (n_b * n_c), (d // n_c) % n_b, d % n_c
            rows = pl.ds(pl.multiple_of(d * cap, cap), cap)
            both = jnp.concatenate([mine[j % 2, rows, :], got[j, rows, :]], axis=0)
            part = jnp.dot(wts[d], both, preferred_element_type=jnp.float32)
            part = part.astype(jnp.bfloat16)
            bufs[0][j % 2, dc, db * n_a + da] = part[:, :half]
            bufs[6][j % 2, db, dc * n_a + da] = part[:, half:]

        for half_index in range(2):
            for copy in sends(half_index, 0, j):
                copy.start()

    def first_sum(j):
        for half_index in range(2):
            (place, side, _), (_, side2, _) = orders[half_index]
            src, dst, nxt = bufs[half_index * 6 : half_index * 6 + 3]
            for copy in sends(half_index, 0, j):
                copy.wait()

            @pl.loop(0, side2 * n_a)
            def _(d):
                total = src[j % 2, place, d].astype(jnp.float32)
                for k in range(side - 1):
                    total += dst[j, k, d].astype(jnp.float32)
                nxt[j % 2, d // n_a, d % n_a] = total.astype(jnp.bfloat16)

            for copy in sends(half_index, 1, j):
                copy.start()

    def second_sum(j):
        for half_index in range(2):
            place, side, _ = orders[half_index][1]
            src, dst, nxt = bufs[half_index * 6 + 2 : half_index * 6 + 5]
            for copy in sends(half_index, 1, j):
                copy.wait()

            @pl.loop(0, n_a)
            def _(d):
                total = src[j % 2, place, d].astype(jnp.float32)
                for k in range(side - 1):
                    total += dst[j, k, d].astype(jnp.float32)
                nxt[j % 2, d] = total.astype(jnp.bfloat16)

            for copy in sends(half_index, 2, j):
                copy.start()

    def last_sum(j):
        for half_index in range(2):
            src, dst = bufs[half_index * 6 + 4 : half_index * 6 + 6]
            for copy in sends(half_index, 2, j):
                copy.wait()
            total = src[j % 2, a].astype(jnp.float32)
            for k in range(n_a - 1):
                total += dst[j, k].astype(jnp.float32)
            columns = pl.ds(pl.multiple_of(j * wide + half_index * half, half), half)
            out[:, columns] = total

    stages = (project, spread, first_sum, second_sum, last_sum)

    @pl.loop(0, chunks + len(stages) - 1)
    def _(step):
        for lag, stage in enumerate(stages):

            @pl.when((step >= lag) & (step - lag < chunks))
            def _():
                stage(step - lag)


def return_call(sides, act, w_out, wts):
    n_a, n_b, n_c = sides
    tok_rows = wts.shape[1]
    slot_rows = act.shape[0] // 2
    half, wide = LANES, 2 * LANES
    block_bytes = tok_rows * half * 2
    chunk_bytes = slot_rows * wide * 2
    for first, second in ((n_c, n_b), (n_b, n_c)):
        chunk_bytes += block_bytes * n_a * (second * (first - 1) + second - 1)
        chunk_bytes += block_bytes * (n_a - 1)
    chunks = w_out.shape[1] // wide
    while chunks % 2 == 0 and chunks * chunk_bytes > VMEM_BUDGET:
        chunks //= 2

    def bf(*shape):
        return pltpu.VMEM(shape, jnp.bfloat16)

    def dma(*shape):
        return pltpu.SemaphoreType.DMA(shape)

    scratch = [bf(2, slot_rows, wide), bf(2, slot_rows, wide), bf(chunks, slot_rows, wide)]
    sems = [dma(2), dma(chunks)]
    for first, second in ((n_c, n_b), (n_b, n_c)):
        scratch += [
            bf(2, first, second * n_a, tok_rows, half),
            bf(chunks, first - 1, second * n_a, tok_rows, half),
            bf(2, second, n_a, tok_rows, half),
            bf(chunks, second - 1, n_a, tok_rows, half),
            bf(2, n_a, tok_rows, half),
            bf(chunks, n_a - 1, tok_rows, half),
        ]
        for side in (first, second, n_a):
            sems += [dma(2, side - 1), dma(chunks, side - 1)]
    piece = chunks * wide
    call = pl.pallas_call(
        functools.partial(return_kernel, sides, chunks),
        out_shape=jax.ShapeDtypeStruct((tok_rows, piece), jnp.float32),
        in_specs=[pl.BlockSpec(memory_space=pltpu.VMEM)] * 3,
        out_specs=pl.BlockSpec(memory_space=pltpu.VMEM),
        scratch_shapes=scratch + sems,
        compiler_params=pltpu.CompilerParams(
            collective_id=0, has_side_effects=True, vmem_limit_bytes=60 * 1024 * 1024
        ),
        name="return_sum",
    )
    parts = [
        call(act, w_out[:, start : start + piece], wts)
        for start in range(0, w_out.shape[1], piece)
    ]
    return parts[0] if len(parts) == 1 else jnp.concatenate(parts, axis=1)


def gather_kernel(sides, chunks, x, info, gains, w_in, act, info_out, *rest):
    (g_a, g_b, info_got, picks, scale, give, mine, got, hid, w_buf) = rest[:10]
    sems = rest[10:]
    n_a, n_b, n_c = sides
    blocks = n_a * n_b * n_c
    seg = lax.axis_index("segment")
    me = lax.axis_index("expert")
    a, b, c = me // (n_b * n_c), (me // n_c) % n_b, me % n_c
    tok_rows, half = x.shape
    part = tok_rows // 2
    wide = half // chunks
    slot_rows = mine.shape[1]
    cap = slot_rows // blocks
    tile = math.gcd(slot_rows, 256)
    units = act.shape[1]
    partner = (1 - seg, me)

    def at(na, nb, nc):
        return (seg, (na * n_b + nb) * n_c + nc)

    def peer_a(k):
        return at((a + k) % n_a, b, c)

    def peer_b(k):
        return at(a, (b + k) % n_b, c)

    def peer_c(k):
        return at(a, b, (c + k) % n_c)

    barrier = pltpu.get_barrier_semaphore()
    pl.semaphore_signal(barrier, inc=1, device_id=partner, device_id_type=MESH)

    @pl.loop(1, blocks)
    def _(k):
        pl.semaphore_signal(
            barrier, inc=1, device_id=(seg, (me + k) % blocks), device_id_type=MESH
        )

    pl.semaphore_wait(barrier, blocks)

    def remote(src, dst, send, recv, peer):
        return pltpu.make_async_remote_copy(
            src_ref=src,
            dst_ref=dst,
            send_sem=send,
            recv_sem=recv,
            device_id=peer,
            device_id_type=MESH,
        )

    def tell(k):
        to = (me + k) % blocks
        return remote(
            info.at[to], info_got.at[me], sems[0].at[k - 1], sems[1].at[k - 1], (seg, to)
        )

    def swap(j):
        return remote(give.at[j % 2], got.at[j], sems[2].at[j % 2], sems[3].at[j], partner)

    orders = (
        (g_a, c, b, n_c, n_b, peer_c, peer_b),
        (g_b, b, c, n_b, n_c, peer_b, peer_c),
    )

    def columns(j):
        return pl.ds(pl.multiple_of(j * wide, wide), wide)

    def sends(which, phase, j, turned=False):
        held, outer, inner, n_outer, n_inner, peer_outer, peer_inner = orders[which]
        send, recv = sems[5 + which * 6 + phase * 2 : 7 + which * 6 + phase * 2]
        if phase == 0:
            src = x.at[pl.ds(which * part, part), columns(j)]
            dst, side, peer = held.at[j, outer, inner, a], n_a, peer_a
            if turned:
                side, peer = n_inner, peer_inner
        elif phase == 1 and turned:
            src = dst = held.at[j, outer, :, a]
            side, peer = n_a, peer_a
        elif phase == 1:
            src = dst = held.at[j, outer, inner]
            side, peer = n_inner, peer_inner
        else:
            src = dst = held.at[j, outer]
            side, peer = n_outer, peer_outer
        return [
            remote(src, dst, send.at[j % 2, k - 1], recv.at[j, k - 1], peer(k))
            for k in range(1, side)
        ]

    def weight_copies(j):
        copies = []
        for which, owner in enumerate((seg, 1 - seg)):
            rows = pl.ds(pl.multiple_of(owner * half + j * wide, wide), wide)
            copies.append(
                pltpu.make_async_copy(
                    w_in.at[rows, :],
                    w_buf.at[j % 2, pl.ds(which * wide, wide)],
                    sems[4].at[j % 2, which],
                )
            )
        return copies

    def each(which, phase, j, action):
        for turned in (False, True):

            @pl.when(j % 3 == 2 if turned else j % 3 != 2)
            def _():
                for copy in sends(which, phase, j, turned):
                    action(copy)

    def first_send(j):
        for which in range(2):
            held, outer, inner = orders[which][:3]
            each(which, 0, j, lambda copy: copy.start())
            held[j, outer, inner, a] = x[pl.ds(which * part, part), columns(j)]

    def relay(phase, j):
        for which in range(2):
            each(which, phase - 1, j, lambda copy: copy.wait())
            each(which, phase, j, lambda copy: copy.start())

    def read_info():
        info_got[me] = info[me]

        @pl.loop(1, blocks)
        def _(k):
            tell(k).wait()

        row = lax.broadcasted_iota(jnp.int32, (cap, tok_rows), 0).astype(jnp.float32)

        @pl.loop(0, blocks)
        def _(d):
            told = info_got[d]
            info_out[d] = told
            own = told[0:1, :] == row
            other = told[1:2, :] == row
            picks[d] = jnp.concatenate(
                [jnp.where(own, 1.0, 0.0), jnp.where(other, 1.0, 0.0)], axis=0
            ).astype(jnp.bfloat16)
            factor = jnp.sum(jnp.where(own, told[4:5, :], 0.0), axis=1, keepdims=True)
            rows = pl.ds(pl.multiple_of(d * cap, cap), cap)
            scale[rows, :] = jnp.broadcast_to(factor, (cap, wide))

    def pick(j):
        for copy in weight_copies(j):
            copy.start()
        for which in range(2):
            for copy in sends(which, 2, j):
                copy.wait()

        @pl.when(j == 0)
        def _():
            read_info()

        @pl.loop(0, blocks, unroll=4)
        def _(d):
            da, db, dc = d // (n_b * n_c), (d // n_c) % n_b, d % n_c
            rows = pl.ds(pl.multiple_of(d * cap, cap), cap)
            there = jnp.concatenate([g_a[j, dc, db, da], g_b[j, db, dc, da]], axis=0)
            taken = jnp.dot(picks[d], there, preferred_element_type=jnp.float32)
            taken = taken.astype(jnp.bfloat16)
            mine[j % 2, rows, :] = taken[:cap]
            give[j % 2, rows, :] = taken[cap:]

        swap(j).start()

    def multiply(j):
        swap(j).wait()
        for copy in weight_copies(j):
            copy.wait()
        places = [
            pl.ds(pl.multiple_of(owner * half + j * wide, wide), wide) for owner in (seg, 1 - seg)
        ]

        @pl.loop(0, slot_rows // tile)
        def _(r):
            rows = pl.ds(pl.multiple_of(r * tile, tile), tile)
            factor = scale[rows, :]
            pieces = [
                ref[rows, :].astype(jnp.float32) * factor for ref in (mine.at[j % 2], got.at[j])
            ]
            for section in range(2):
                normed = jnp.concatenate(
                    [
                        (piece * gains[pl.ds(section, 1), place]).astype(jnp.bfloat16)
                        for piece, place in zip(pieces, places)
                    ],
                    axis=1,
                )
                to = pl.ds(pl.multiple_of(section * slot_rows + r * tile, tile), tile)
                hid[to, :] += jnp.dot(
                    normed, w_buf[j % 2], preferred_element_type=jnp.float32
                )

    @pl.loop(1, blocks)
    def _(k):
        tell(k).start()

    stages = (
        first_send,
        functools.partial(relay, 1),
        functools.partial(relay, 2),
        pick,
        multiply,
    )

    @pl.loop(0, chunks + len(stages) - 1)
    def _(step):
        for lag, stage in enumerate(stages):

            @pl.when((step >= lag) & (step - lag < chunks))
            def _():
                stage(step - lag)

        @pl.when(step == 0)
        def _():
            @pl.loop(0, 2 * slot_rows // tile)
            def _(r):
                rows = pl.ds(pl.multiple_of(r * tile, tile), tile)
                hid[rows, :] = jnp.zeros((tile, 2 * units), jnp.float32)

    @pl.loop(0, 2 * slot_rows // tile)
    def _(r):
        rows = pl.ds(pl.multiple_of(r * tile, tile), tile)
        gate = hid[rows, :units]
        act[rows, :] = (gate / (1.0 + jnp.exp(-gate)) * hid[rows, units:]).astype(jnp.bfloat16)


def gather_call(sides, room, x, info, gains, w_in):
    n_a, n_b, n_c = sides
    blocks = n_a * n_b * n_c
    tok_rows, half = x.shape
    wide = LANES
    chunks = half // wide
    slot_rows = blocks * room
    units = w_in.shape[1] // 2
    part = tok_rows // 2

    def bf(*shape):
        return pltpu.VMEM(shape, jnp.bfloat16)

    def f32(*shape):
        return pltpu.VMEM(shape, jnp.float32)

    def dma(*shape):
        return pltpu.SemaphoreType.DMA(shape)

    scratch = [
        bf(chunks, n_c, n_b, n_a, part, wide),
        bf(chunks, n_b, n_c, n_a, part, wide),
        f32(*info.shape),
        bf(blocks, 2 * room, tok_rows),
        f32(slot_rows, wide),
        bf(2, slot_rows, wide),
        bf(2, slot_rows, wide),
        bf(chunks, slot_rows, wide),
        f32(2 * slot_rows, 2 * units),
        bf(2, 2 * wide, 2 * units),
    ]
    sems = [dma(blocks - 1), dma(blocks - 1), dma(2), dma(chunks), dma(2, 2)]
    for outer, inner in ((n_c, n_b), (n_b, n_c)):
        for side in (max(n_a, inner), max(n_a, inner), outer):
            sems += [dma(2, side - 1), dma(chunks, side - 1)]
    vmem = pl.BlockSpec(memory_space=pltpu.VMEM)
    return pl.pallas_call(
        functools.partial(gather_kernel, sides, chunks),
        out_shape=(
            jax.ShapeDtypeStruct((2 * slot_rows, units), jnp.bfloat16),
            jax.ShapeDtypeStruct(info.shape, jnp.float32),
        ),
        in_specs=[vmem, vmem, vmem, pl.BlockSpec(memory_space=pl.ANY)],
        out_specs=(vmem, vmem),
        scratch_shapes=scratch + sems,
        compiler_params=pltpu.CompilerParams(
            collective_id=1, has_side_effects=True, vmem_limit_bytes=60 * 1024 * 1024
        ),
        name="gather_hidden",
    )(x, info, gains, w_in)


def swap_cores(x):
    count = lax.axis_size("segment")
    return lax.ppermute(x, "segment", [(i, count - 1 - i) for i in range(count)])


def inverse_rms(values):
    return lax.rsqrt(jnp.mean(values * values, axis=-1, keepdims=True) + 1e-06)


def per_device(
    rollout,
    norm_gain,
    router_first,
    gain_second,
    router_second,
    expert_ids,
    copy_pick,
    later_ids,
    slot_table,
    expert_in,
    expert_out,
):
    position = lax.axis_index("segment")
    segment_count = lax.axis_size("segment")
    chip_count = lax.axis_size("expert")
    tok_rows, half = rollout.shape
    top_count = expert_ids.shape[1]
    experts_all = router_first.shape[2]
    slot_count = slot_table.shape[0]
    capacity = 3 * tok_rows * top_count // (2 * segment_count * chip_count)

    expert_cols = jnp.arange(experts_all, dtype=jnp.int32)
    slot_ids = jnp.arange(slot_count, dtype=jnp.int32)
    same = slot_table[:, None] == slot_table[None, :]
    earlier = slot_ids[:, None] < slot_ids[None, :]
    copy_rank = jnp.sum((same & earlier).astype(jnp.int32), axis=0)
    slot_holders = jnp.sum(same.astype(jnp.int32), axis=0)
    here = slot_table == expert_ids[..., None]
    copies = jnp.max(jnp.where(here, slot_holders, 1), axis=-1)
    wanted = copy_pick % copies
    match = here & (copy_rank == wanted[..., None])
    hit = jnp.sum(match.astype(jnp.bfloat16), axis=1)
    order = jnp.arange(tok_rows, dtype=jnp.int32)
    before_mask = (order[None, :] < order[:, None]).astype(jnp.bfloat16)
    before = jnp.dot(before_mask, hit, preferred_element_type=jnp.float32).astype(jnp.int32)
    other_half = swap_cores(rollout)
    first = position == 0
    left = jnp.where(first, rollout, other_half)
    right = jnp.where(first, other_half, rollout)
    whole = jnp.concatenate([left, right], axis=1)
    states_in = whole.astype(jnp.float32)
    factor = inverse_rms(states_in)
    normed = (states_in * factor * norm_gain[0].astype(jnp.float32)).astype(
        jnp.bfloat16
    )
    logits = jnp.dot(normed, router_first[0], preferred_element_type=jnp.float32)
    picked = expert_ids[..., None] == expert_cols
    chosen = jnp.sum(jnp.where(picked, logits[:, None, :], 0.0), axis=-1)
    lifted = jnp.exp(chosen - jnp.max(chosen, axis=1, keepdims=True))
    gates = (lifted / jnp.sum(lifted, axis=1, keepdims=True)).astype(jnp.bfloat16)
    place = jnp.where((hit > 0) & (before < capacity), before, -1).astype(jnp.float32)
    gate = jnp.sum(jnp.where(match, gates.astype(jnp.float32)[..., None], 0.0), axis=1)

    def by_core(values):
        cores = values.T.reshape(segment_count, chip_count, tok_rows)
        own = jnp.where(first, cores[0], cores[1])
        other = jnp.where(first, cores[1], cores[0])
        return [own, other]

    factors = jnp.broadcast_to(factor[:, 0], (chip_count, tok_rows))
    blank = jnp.zeros((chip_count, tok_rows), jnp.float32)
    info = jnp.stack(by_core(place) + by_core(gate) + [factors, blank, blank, blank], axis=1)
    gains = jnp.concatenate([swap_cores(norm_gain), norm_gain], axis=0).astype(jnp.float32)
    room = -(-capacity // 16) * 16
    sides = grid_sides(chip_count)
    active, told = gather_call(sides, room, rollout, info, gains, expert_in[0])
    rows = jnp.arange(room, dtype=jnp.float32)

    def spread(place, weight):
        return jnp.where(place[..., None] == rows, weight[..., None], 0.0).astype(jnp.bfloat16)

    weights = jnp.concatenate(
        [spread(told[:, 0], told[:, 2]), spread(told[:, 1], told[:, 3])], axis=2
    )
    summed = return_call(sides, active, expert_out[0], weights)
    mixed = states_in + summed
    later = (mixed * inverse_rms(mixed) * gain_second[0].astype(jnp.float32)).astype(jnp.bfloat16)
    logp = jax.nn.log_softmax(
        jnp.dot(later, router_second[0], preferred_element_type=jnp.float32), axis=-1
    )
    later_pick = later_ids[..., None] == expert_cols
    score = jnp.sum(jnp.where(later_pick, logp[:, None, :], 0.0), axis=(1, 2))
    partner = swap_cores(score)
    ratio = jnp.where(position == 1, score - partner, partner - score)
    paired = ratio.reshape(tok_rows // 2, 2)
    column = lax.dynamic_slice_in_dim(paired, position, 1, 1)
    return (mixed.astype(jnp.bfloat16)[None], column)


def solution(mesh):
    in_specs = (
        P("expert", "segment"),
        P("segment", None),
        P("segment", None, None),
        P("segment", None),
        P("segment", None, None),
        P("expert", None),
        P("expert", None),
        P("expert", None),
        P(),
        P(("segment", "expert"), None, None),
        P(("segment", "expert"), None, None),
    )
    out_specs = (P("segment", "expert", None), P("expert", "segment"))
    return jax.shard_map(
        per_device, mesh=mesh, in_specs=in_specs, out_specs=out_specs, check_vma=False
    )
```
